32 devices in a mesh: gx: 4 (over y, core), gy: 8 (over z, x).
Axes of the slice: x: 2, y: 2, z: 4, core: 2. Of those that a mesh axis runs over, the one named last changes fastest.
Arguments:
- features: bfloat16 [4, 8, 128, 256], P('gx', 'gy'), may hold values from -6 to 6
- occupancy: int32 [4, 8, 128], P('gx', 'gy'), may hold values from 0 to 1, as said below
- coords: int32 [4, 8, 3, 128], P('gx', 'gy'), may hold values from 0 to 7, as said below
- norm_gains: float32 [2, 2, 256], replicated, may hold values from 0.1 to 1.9
- bias_tables: float32 [2, 3, 8, 15], replicated, may hold values from -4 to 4
- w_qkv: bfloat16 [2, 256, 768], replicated, may hold values from -0.375 to 0.375
- w_out: bfloat16 [2, 256, 256], replicated, may hold values from -0.375 to 0.375
- w_up: bfloat16 [2, 256, 1024], replicated, may hold values from -0.375 to 0.375
- w_down: bfloat16 [2, 1024, 256], replicated, may hold values from -0.1875 to 0.1875
- grad_out: bfloat16 [4, 8, 128, 256], P('gx', 'gy'), may hold values from -6 to 6
Outputs:
- out_points: bfloat16 [4, 8, 128, 256], P('gx', 'gy')
- grad_points: bfloat16 [4, 8, 128, 256], P('gx', 'gy')
- grad_tables: float32 [2, 3, 8, 15], replicated
The draws below stay inside these ranges and needn't reach their ends.
Inputs may be any that keep to these rules, and one draw needn't show every extreme that they name: `occupancy`: 1 marks an occupied slot. In each quarter of 32 slots of a window the occupied slots come first, and every quarter holds at least one. `coords`: the x coordinate of a slot of quarter (a, b) lies in [a * 4, (a + 1) * 4) and its y coordinate in [b * 4, (b + 1) * 4); z lies in [0, 8).
All inputs are finite; a program needn't handle non-finite values.
Results may differ from the reference program's by a relative error of at most 0.02.
Values may be sent and summed in bfloat16 or wider, within the bound.
A program may use at most 64 MiB of HBM per device.

```python
from functools import partial
import jax
import jax.numpy as jnp
from jax import lax

C = 256
HEADS = 8
FF = 1024
SLOTS = 128
QUAD = 32
WS = 8
NREL = 15
NWX = 4
NWY = 8


def draw_occupancy(key, part):
    level_key, count_key = jax.random.split(key)
    levels = jax.random.randint(level_key, (NWX, NWY, 1), 0, 4)
    lower = levels * (QUAD // 4) + 1
    upper = jnp.minimum((levels + 2) * (QUAD // 4), QUAD) + 1
    counts = jax.random.randint(count_key, (NWX, NWY, 4), lower, upper)
    slot_rank = jnp.arange(QUAD, dtype=jnp.int32)
    filled = (slot_rank[None, None, None, :] < counts[..., None]).astype(jnp.int32)
    return filled.reshape(NWX, NWY, SLOTS)


def draw_coords(key, part):
    half_span = WS // 2
    slot_index = jnp.arange(SLOTS, dtype=jnp.int32)
    upper_x = slot_index // (2 * QUAD)
    upper_y = slot_index // QUAD % 2
    keys_three = jax.random.split(jax.random.fold_in(key, 7), 3)
    within_x = jax.random.randint(keys_three[0], (NWX, NWY, SLOTS), 0, half_span)
    within_y = jax.random.randint(keys_three[1], (NWX, NWY, SLOTS), 0, half_span)
    coord_z = jax.random.randint(keys_three[2], (NWX, NWY, SLOTS), 0, WS)
    coord_x = upper_x[None, None, :] * half_span + within_x
    coord_y = upper_y[None, None, :] * half_span + within_y
    return jnp.stack([coord_x, coord_y, coord_z], axis=2).astype(jnp.int32)


def level_of(own_key, extent, cuts, smallest, top_value):
    loudness, own = 1.0, jax.random.fold_in(own_key, 6)
    for dim, blocks in cuts:
        heights = jnp.exp(jax.random.uniform(jax.random.fold_in(own, dim), (blocks,), jnp.float32, smallest / len(cuts), top_value / len(cuts)))
        loudness = loudness * jnp.repeat(heights, extent[dim] // blocks).reshape([-1 if axis == dim else 1 for axis in range(len(extent))])
    return loudness


def scatter_about(own_key, dims, scale, reach, pieces=(), kind=jnp.bfloat16):
    values = scale * jax.random.normal(own_key, dims, jnp.float32)
    if pieces:
        values = values * level_of(own_key, dims, pieces, -0.22, 0.18)
    return jnp.clip(values, -reach, reach).astype(kind)


def setup_inputs(seed: int = 0) -> dict:
    seeds = jax.random.split(jax.random.key(seed), 11)
    features = scatter_about(seeds[0], (NWX, NWY, SLOTS, C), 1.0, 6.0, ((0, 4), (1, 8)))
    occupancy = draw_occupancy(jax.random.fold_in(seeds[10], 71), 0)
    coords = draw_coords(jax.random.fold_in(seeds[10], 71), 0)
    norm_gains = jnp.clip(1.0 + 0.18 * jax.random.normal(seeds[3], (2, 2, C), jnp.float32), 0.1, 1.9)
    bias_tables = scatter_about(seeds[4], (2, 3, HEADS, NREL), 1.0, 4.0, (), jnp.float32)
    w_qkv = scatter_about(seeds[5], (2, C, 3 * C), C ** -0.5, 0.375)
    w_out = scatter_about(seeds[6], (2, C, C), C ** -0.5, 0.375)
    w_up = scatter_about(seeds[7], (2, C, FF), C ** -0.5, 0.375)
    w_down = scatter_about(seeds[8], (2, FF, C), FF ** -0.5, 0.1875)
    grad_out = scatter_about(seeds[9], (NWX, NWY, SLOTS, C), 1.0, 6.0, ((0, 4), (1, 8)))
    return dict(features=features, occupancy=occupancy, coords=coords, norm_gains=norm_gains, bias_tables=bias_tables, w_qkv=w_qkv, w_out=w_out, w_up=w_up, w_down=w_down, grad_out=grad_out)


highest_precision = lax.Precision.HIGHEST
epsilon = 1e-05

def layer_norm(values, gain):
    mean_value = lax.optimization_barrier(jnp.mean(values, axis=-1, keepdims=True))
    centred = values - mean_value
    variance = lax.optimization_barrier(jnp.mean(centred * centred, axis=-1, keepdims=True))
    return centred * lax.rsqrt(variance + epsilon) * gain

def relative_bias(coords, bias_table):
    table_span = bias_table.shape[-1]
    window_span = (table_span + 1) // 2
    cell_index = jnp.arange(window_span, dtype=jnp.int32)
    offsets = cell_index[:, None] - cell_index[None, :] + window_span - 1
    selection_matrix = (offsets[:, :, None] == jnp.arange(table_span, dtype=jnp.int32)[None, None, :]).astype(jnp.float32)
    total = None
    for axis_index in range(3):
        indicator_matrix = (coords[axis_index][:, None] == cell_index[None, :]).astype(jnp.float32)
        banded_offset_matrix = jnp.einsum('hr,abr->hab', bias_table[axis_index], selection_matrix, precision=highest_precision)
        left_factor = jnp.einsum('dx,cxq->cdq', indicator_matrix, banded_offset_matrix, precision=highest_precision)
        axis_contribution_part = jnp.einsum('klu,tu->klt', left_factor, indicator_matrix, precision=highest_precision)
        total = axis_contribution_part if total is None else total + axis_contribution_part
    return total

def attend(queries, keys_part, values_part, bias_table, occupied, coords):
    head_size = queries.shape[-1]
    scores = jnp.einsum('qhd,khd->hqk', queries.astype(jnp.float32), keys_part.astype(jnp.float32), precision=highest_precision)
    scores = scores * head_size ** (-0.5) + relative_bias(coords, bias_table)
    scores = jnp.where(occupied[None, None, :] > 0, scores, -1e+30)
    weights_soft = jax.nn.softmax(scores, axis=-1).astype(jnp.bfloat16)
    mixed = jnp.einsum('hqk,khd->qhd', weights_soft.astype(jnp.float32), values_part.astype(jnp.float32), precision=highest_precision)
    return mixed.reshape(mixed.shape[0], -1).astype(jnp.bfloat16)

def swin_block(hidden, bias_table, occupied, coords, gains, weight_qkv, weight_out, up_weight_matrix, weight_down):
    slots, width = hidden.shape
    heads = bias_table.shape[1]
    core = jax.checkpoint(partial(attend, occupied=occupied, coords=coords))
    normed = layer_norm(hidden.astype(jnp.float32), gains[0]).astype(jnp.bfloat16)
    projected = jnp.dot(normed, weight_qkv, preferred_element_type=jnp.float32).astype(jnp.bfloat16)
    qkv_parts = projected.reshape(slots, 3, heads, width // heads)
    mixed = core(qkv_parts[:, 0], qkv_parts[:, 1], qkv_parts[:, 2], bias_table)
    middle = hidden.astype(jnp.float32) + jnp.dot(mixed, weight_out, preferred_element_type=jnp.float32)
    normed_two = layer_norm(middle, gains[1]).astype(jnp.bfloat16)
    expanded = jax.nn.gelu(jnp.dot(normed_two, up_weight_matrix, preferred_element_type=jnp.float32)).astype(jnp.bfloat16)
    return (middle + jnp.dot(expanded, weight_down, preferred_element_type=jnp.float32)).astype(jnp.bfloat16)

def roll_grid(array, shift_count):
    count_x, count_y = (array.shape[0], array.shape[1])
    trailing = array.shape[4:]
    quarter_grid = jnp.swapaxes(array, 1, 2).reshape((2 * count_x, 2 * count_y) + trailing)
    quarter_grid = jnp.roll(quarter_grid, (shift_count, shift_count), axis=(0, 1))
    return jnp.swapaxes(quarter_grid.reshape((count_x, 2, count_y, 2) + trailing), 1, 2)

def roll_points(points, shift_count):
    count_x, count_y, slots, width = points.shape
    tiles = points.reshape(count_x, count_y, 2, 2, slots // 4, width)
    return roll_grid(tiles, shift_count).reshape(points.shape)

def reference(features, occupancy, coords, norm_gains, bias_tables, w_qkv, w_out, w_up, w_down, grad_out):
    count_x, count_y, slots, width = features.shape
    quarter = slots // 4
    window_span = (bias_tables.shape[-1] + 1) // 2
    half_span = window_span // 2
    slot_meta = jnp.concatenate([occupancy[:, :, None, :], coords], axis=2)
    meta_tiles = jnp.moveaxis(slot_meta.reshape(count_x, count_y, 4, 2, 2, quarter), 2, -1)
    meta_tiles = jnp.moveaxis(roll_grid(meta_tiles, -1), -1, 2).reshape(count_x, count_y, 4, slots)
    shifted_coords = jnp.stack([(meta_tiles[:, :, 1] + half_span) % window_span, (meta_tiles[:, :, 2] + half_span) % window_span, meta_tiles[:, :, 3]], axis=2)
    occupied = occupancy.astype(jnp.float32)
    shifted_occupied = meta_tiles[:, :, 0].astype(jnp.float32)
    occupied_mask = occupancy.astype(jnp.bfloat16)[..., None]

    def apply_windows(points, bias_table, occupied_in, coords_in, block_index):

        def one_window(packed):
            return swin_block(packed[0], bias_table, packed[1], packed[2], norm_gains[block_index], w_qkv[block_index], w_out[block_index], w_up[block_index], w_down[block_index])
        per_window = lax.map(one_window, (points.reshape(-1, slots, width), occupied_in.reshape(-1, slots), coords_in.reshape(-1, 3, slots)))
        return per_window.reshape(points.shape)

    def run_blocks(points, tables):
        first_out = apply_windows(points, tables[0], occupied, coords, 0)
        second = apply_windows(roll_points(first_out, -1), tables[1], shifted_occupied, shifted_coords, 1)
        return roll_points(second, 1) * occupied_mask
    out_points, pullback = jax.vjp(run_blocks, features, bias_tables)
    grad_points, grad_tables = pullback(grad_out)
    return (out_points, grad_points, grad_tables)
```

```python
from functools import partial

import jax
import jax.numpy as jnp
from jax import lax
from jax.experimental import pallas as pl
from jax.experimental.pallas import tpu as pltpu
from jax.sharding import PartitionSpec as P

EPSILON = 1e-05
GELU_SCALE = 0.7978845608028654
GELU_CUBE = 0.044715
MESH = pl.DeviceIdType.MESH
F32 = jnp.float32
BF16 = jnp.bfloat16


def dot_nn(a, b):
    return jnp.dot(a, b, preferred_element_type=F32)


def dot_nt(a, b):
    return lax.dot_general(a, b, (((1,), (1,)), ((), ())), preferred_element_type=F32)


def norm_parts(values):
    mean_value = jnp.mean(values, axis=-1, keepdims=True)
    centred = values - mean_value
    variance = jnp.mean(centred * centred, axis=-1, keepdims=True)
    scale = lax.rsqrt(variance + EPSILON)
    return centred * scale, scale


def norm_pullback(cotangent, gain, unit, scale):
    inner = cotangent * gain
    first = jnp.mean(inner, axis=-1, keepdims=True)
    second = jnp.mean(inner * unit, axis=-1, keepdims=True)
    return scale * (inner - first - unit * second)


def split_two(values):
    high = values.astype(BF16)
    return high, (values - high.astype(F32)).astype(BF16)


def kernel(
    nx, ny,
    feat, occ, coords, gains, tables, wqkv, wout, wup, wdown, gout,
    out_points, grad_points, grad_tables,
    x_v, g_v, wqkv_v, wout_v, wup_v, wdown_v,
    meta, meta_recv, g_roll, first, rolled, second, back, grad_mid, grad_first,
    table_pad, band, left_bias, diag, probs, proj, keys_t, unit_one, unit_two,
    rstd_one, rstd_two, gelu_in, onehot_s, onehot_t, score_cot, q_stack, mix_stack,
    t_send, t_recv_x, t_mid, t_recv_y,
    load_sem, send_sem, recv_sem, tx_send, tx_recv, ty_send, ty_recv,
):
    slots, width = x_v.shape
    quarter = slots // 4
    heads = tables.shape[2]
    span = tables.shape[3]
    cells = (span + 1) // 2
    half = cells // 2
    head_size = width // heads
    scale = head_size ** -0.5
    i = lax.axis_index("gx")
    j = lax.axis_index("gy")
    up_i, down_i = lax.rem(i + 1, nx), lax.rem(i + nx - 1, nx)
    up_j, down_j = lax.rem(j + 1, ny), lax.rem(j + ny - 1, ny)

    barrier = pltpu.get_barrier_semaphore()
    for step in range(1, nx):
        pl.semaphore_signal(barrier, 1, device_id=(lax.rem(i + step, nx), j), device_id_type=MESH)
    for step in range(1, ny):
        pl.semaphore_signal(barrier, 1, device_id=(i, lax.rem(j + step, ny)), device_id_type=MESH)
    pl.semaphore_signal(barrier, 1, device_id=(up_i, up_j), device_id_type=MESH)
    pl.semaphore_signal(barrier, 1, device_id=(down_i, down_j), device_id_type=MESH)

    pairs = [(feat.at[0, 0], x_v)]
    for k in range(2):
        pairs += [
            (wqkv.at[k], wqkv_v.at[k]),
            (wout.at[k], wout_v.at[k]),
            (wup.at[k], wup_v.at[k]),
            (wdown.at[k], wdown_v.at[k]),
        ]
    pairs.append((gout.at[0, 0], g_v))
    loads = [pltpu.make_async_copy(a, b, load_sem.at[n]) for n, (a, b) in enumerate(pairs)]
    for load in loads:
        load.start()

    def remote(source, target, place, device):
        return pltpu.make_async_remote_copy(
            src_ref=source, dst_ref=target, send_sem=send_sem.at[place],
            recv_sem=recv_sem.at[place], device_id=device, device_id_type=MESH,
        )

    def rows(number):
        return pl.ds(number * quarter, quarter)

    def roll_forward(source, target, base):
        copies = [
            remote(source.at[rows(0)], target.at[rows(3)], base, (down_i, down_j)),
            remote(source.at[rows(1)], target.at[rows(2)], base + 1, (down_i, j)),
            remote(source.at[rows(2)], target.at[rows(1)], base + 2, (i, down_j)),
        ]
        for copy in copies:
            copy.start()
        target[rows(0)] = source[rows(3)]
        return copies

    def roll_backward(source, target, base):
        copies = [
            remote(source.at[rows(3)], target.at[rows(0)], base, (up_i, up_j)),
            remote(source.at[rows(2)], target.at[rows(1)], base + 1, (up_i, j)),
            remote(source.at[rows(1)], target.at[rows(2)], base + 2, (i, up_j)),
        ]
        for copy in copies:
            copy.start()
        target[rows(3)] = source[rows(0)]
        return copies

    lane = lax.broadcasted_iota(jnp.int32, (heads, slots), 1)
    lane_row = lax.broadcasted_iota(jnp.int32, (1, slots), 1)
    channel = lax.broadcasted_iota(jnp.int32, (1, width), 1)
    head_masks = [
        ((channel >= h * head_size) & (channel < (h + 1) * head_size)).astype(F32).astype(BF16)
        for h in range(heads)
    ]
    pad_rows = 32

    def prepare_bias(k, occupied_row, coord_rows):
        cell = lax.broadcasted_iota(jnp.int32, (cells, slots), 0)
        blocks = [(jnp.broadcast_to(c, (cells, slots)) == cell).astype(F32) for c in coord_rows]
        empty = jnp.zeros((cells, slots), F32)
        first_row = cell == 0
        mask_block = jnp.where(
            first_row, jnp.broadcast_to(occupied_row.astype(F32) - 1.0, (cells, slots)), 0.0
        )
        one_block = jnp.where(first_row, 1.0, 0.0)
        rest = jnp.zeros((slots - 2 * pad_rows, slots), F32)
        right = jnp.concatenate(
            blocks + [one_block] + blocks + [empty, rest], axis=0
        ).astype(BF16)
        left = jnp.concatenate(blocks + [mask_block, empty, empty, empty, empty, rest], axis=0)
        left_t = jnp.transpose(left)
        onehot_s[k] = left_t.astype(BF16)
        onehot_t[k] = jnp.concatenate(blocks + [empty], axis=0).astype(BF16)
        table_pad[...] = jnp.zeros_like(table_pad)
        for e in range(3):
            table_pad[e, :, 0:span] = tables[k, e]
        mask_row = jnp.where(lane == 3 * cells, 1e30, 0.0)
        for u in range(cells):
            row = mask_row if u == 0 else jnp.zeros_like(mask_row)
            band[pl.ds(3 * cells + u, heads, stride=pad_rows), :] = row
        for e in range(3):
            padded = table_pad[e]
            inside = (lane >= e * cells) & (lane < (e + 1) * cells)
            for u in range(cells):
                shift = (e * cells + u - (cells - 1)) % slots
                moved = pltpu.roll(padded, shift, 1) if shift else padded
                tile = jnp.where(inside, moved, 0.0)
                high = tile.astype(BF16).astype(F32)
                tile = high + pltpu.roll(tile - high, pad_rows, 1)
                band[pl.ds(e * cells + u, heads, stride=pad_rows), :] = tile
        left_hot = onehot_s[k][:, 0:pad_rows]
        for h in range(heads):
            banded = band[h * pad_rows:(h + 1) * pad_rows, :].astype(BF16)
            factor = dot_nn(left_hot, banded).astype(BF16)
            left_bias[k, h] = dot_nn(factor, right)
        return left_t[:, 3 * cells:3 * cells + 1] + 1.0

    def attention_part(k, hidden):
        unit, rstd = norm_parts(hidden)
        unit_one[k] = unit
        rstd_one[k] = rstd
        normed = (unit * gains[k, 0:1]).astype(BF16)
        loads[1 + 4 * k].wait()
        projected = dot_nn(normed, wqkv_v[k])
        proj[k] = projected.astype(BF16)
        keys_t[k] = jnp.transpose(projected[:, width:2 * width]).astype(BF16)
        values_t = jnp.transpose(projected[:, 2 * width:]).astype(BF16)
        queries = proj[k, :, 0:width]
        keys = proj[k, :, width:2 * width]
        pieces = []
        for h in range(heads):
            scores = dot_nt(keys * head_masks[h], queries) * scale + left_bias[k, h]
            top = jnp.max(scores, axis=0, keepdims=True)
            powers = jnp.exp(scores - top)
            weights = (powers * (1.0 / jnp.sum(powers, axis=0, keepdims=True))).astype(BF16)
            probs[k, h] = weights
            pieces.append(dot_nn(values_t[h * head_size:(h + 1) * head_size], weights))
        mixed = jnp.transpose(jnp.concatenate(pieces, axis=0)).astype(BF16)
        loads[2 + 4 * k].wait()
        return hidden + dot_nn(mixed, wout_v[k])

    def feed_part(k, middle):
        unit, rstd = norm_parts(middle)
        unit_two[k] = unit
        rstd_two[k] = rstd
        normed = (unit * gains[k, 1:2]).astype(BF16)
        loads[3 + 4 * k].wait()
        wide = dot_nn(normed, wup_v[k])
        gelu_in[k] = wide
        inner = jnp.tanh(GELU_SCALE * (wide + GELU_CUBE * (wide * wide * wide)))
        expanded = (0.5 * wide * (1.0 + inner)).astype(BF16)
        loads[4 + 4 * k].wait()
        return (middle + dot_nn(expanded, wdown_v[k])).astype(BF16)

    def gelu_slope(k):
        wide = gelu_in[k]
        square = wide * wide
        inner = jnp.tanh(GELU_SCALE * (wide + GELU_CUBE * (square * wide)))
        gelu_in[k] = 0.5 * (1.0 + inner) + (0.5 * GELU_SCALE) * wide * (1.0 - inner * inner) * (
            1.0 + (3.0 * GELU_CUBE) * square
        )

    def block_pullback(k, cotangent, with_tables):
        cot_wide = dot_nt(cotangent, wdown_v[k]).astype(BF16).astype(F32) * gelu_in[k]
        cot_normed = dot_nt(cot_wide.astype(BF16), wup_v[k]).astype(BF16).astype(F32)
        cot_middle = cotangent.astype(F32) + norm_pullback(
            cot_normed, gains[k, 1:2], unit_two[k], rstd_two[k]
        )
        cot_mixed = dot_nt(cot_middle.astype(BF16), wout_v[k]).astype(BF16)
        queries = proj[k, :, 0:width]
        values = proj[k, :, 2 * width:]
        hot_twice = jnp.concatenate([onehot_s[k], onehot_s[k]], axis=0)
        hot_t_twice = jnp.concatenate([onehot_t[k], onehot_t[k]], axis=1)
        pieces, tile_list = [], []
        for h in range(heads):
            here = pl.ds(h * slots, slots)
            cot_probs = dot_nt(values * head_masks[h], cot_mixed).astype(BF16).astype(F32)
            weights = probs[k, h].astype(F32)
            product = weights * cot_probs
            total = jnp.sum(product, axis=0, keepdims=True)
            cot_scores = product - weights * total
            high, low = split_two(cot_scores)
            pieces.append(dot_nn(keys_t[k, h * head_size:(h + 1) * head_size], high))
            score_cot[:, here] = high
            q_stack[here, :] = queries * head_masks[h]
            mix_stack[here, :] = cot_mixed * head_masks[h]
            by_key = dot_nn(jnp.concatenate([high, low], axis=1), hot_twice)
            key_high, key_low = split_two(by_key)
            diag[h * pad_rows:(h + 1) * pad_rows, :] = dot_nn(
                hot_t_twice, jnp.concatenate([key_high, key_low], axis=0)
            )
        sums = jnp.zeros((heads, slots), F32)
        for e in range(3):
            inside = (lane >= e * cells) & (lane < (e + 1) * cells)
            for u in range(cells):
                tile = jnp.where(inside, diag[pl.ds(e * cells + u, heads, stride=pad_rows), :], 0.0)
                shift = e * cells + (cells - 1) - u
                sums = sums + (pltpu.roll(tile, shift, 1) if shift else tile)
        t_send[k * heads:(k + 1) * heads, :] = sums
        with_tables()
        cot_queries = (jnp.transpose(jnp.concatenate(pieces, axis=0)) * scale).astype(BF16)
        cot_keys = (dot_nn(score_cot[...], q_stack[...]) * scale).astype(BF16)
        probs_wide = jnp.concatenate([probs[k, h] for h in range(heads)], axis=1)
        cot_values = dot_nn(probs_wide, mix_stack[...]).astype(BF16)
        cot_proj = jnp.concatenate([cot_queries, cot_keys, cot_values], axis=1)
        cot_normed = dot_nt(cot_proj, wqkv_v[k]).astype(BF16).astype(F32)
        return (
            cot_middle + norm_pullback(cot_normed, gains[k, 0:1], unit_one[k], rstd_one[k])
        ).astype(BF16)

    meta[...] = jnp.zeros_like(meta)
    meta[0:1, :] = occ[0]
    meta[1:4, :] = coords[0, 0]
    occupied = prepare_bias(0, occ[0], [coords[0, 0, e:e + 1] for e in range(3)])
    loads[0].wait()
    middle = attention_part(0, x_v[...].astype(F32))

    pl.semaphore_wait(barrier, nx + ny)
    meta_copies = [
        remote(meta, meta_recv.at[0], 0, (down_i, down_j)),
        remote(meta, meta_recv.at[1], 1, (down_i, j)),
        remote(meta, meta_recv.at[2], 2, (i, down_j)),
    ]
    for copy in meta_copies:
        copy.start()
    loads[9].wait()
    grad_copies = roll_forward(g_v, g_roll, 3)

    first[...] = feed_part(0, middle)
    first_copies = roll_forward(first, rolled, 6)

    for copy in meta_copies:
        copy.wait()
    own = pltpu.roll(meta[...], quarter, 1)
    from_y = pltpu.roll(meta_recv[2], slots - quarter, 1)
    from_x = pltpu.roll(meta_recv[1], quarter, 1)
    from_xy = pltpu.roll(meta_recv[0], slots - quarter, 1)
    moved = jnp.where(
        lane_row < quarter, own,
        jnp.where(lane_row < 2 * quarter, from_y, jnp.where(lane_row < 3 * quarter, from_x, from_xy)),
    )

    def wrapped(values):
        moved_on = values + half
        return jnp.where(moved_on >= cells, moved_on - cells, moved_on)

    shifted_occupied = prepare_bias(
        1, moved[0:1], [wrapped(moved[1:2]), wrapped(moved[2:3]), moved[3:4]]
    )
    gelu_slope(0)
    for copy in first_copies:
        copy.wait()
    middle = attention_part(1, rolled[...].astype(F32))
    second[...] = feed_part(1, middle)
    second_copies = roll_backward(second, back, 9)
    gelu_slope(1)
    for copy in grad_copies:
        copy.wait()
    grad_in = (g_roll[...].astype(F32) * shifted_occupied).astype(BF16)
    grad_mid[...] = block_pullback(1, grad_in, lambda: None)
    mid_copies = roll_backward(grad_mid, grad_first, 12)
    for copy in second_copies:
        copy.wait()
    out_points[0, 0] = (back[...].astype(F32) * occupied).astype(BF16)
    for copy in mid_copies:
        copy.wait()

    def exchange(source, target, send, recv, me, count, device_of):
        copies = []
        for step in range(1, count):
            copies.append(
                pltpu.make_async_remote_copy(
                    src_ref=source, dst_ref=target.at[me], send_sem=send.at[step],
                    recv_sem=recv.at[step], device_id=device_of(lax.rem(me + step, count)),
                    device_id_type=MESH,
                )
            )
            copies[-1].start()
        target[me] = source[...]
        return copies

    table_copies = []

    def send_tables():
        table_copies.extend(
            exchange(t_send, t_recv_x, tx_send, tx_recv, i, nx, lambda other: (other, j))
        )

    grad_points[0, 0] = block_pullback(0, grad_first[...], send_tables)
    for copy in table_copies:
        copy.wait()
    total = t_recv_x[0]
    for n in range(1, nx):
        total = total + t_recv_x[n]
    t_mid[...] = total
    for copy in exchange(t_mid, t_recv_y, ty_send, ty_recv, j, ny, lambda other: (i, other)):
        copy.wait()
    total = t_recv_y[0]
    for n in range(1, ny):
        total = total + t_recv_y[n]
    for k in range(2):
        for e in range(3):
            tile = total[k * heads:(k + 1) * heads]
            shift = (slots - 2 * cells * e) % slots
            tile = pltpu.roll(tile, shift, 1) if shift else tile
            grad_tables[k, e] = tile[:, 0:span]


def on_device(
    nx, ny, features, occupancy, coords, norm_gains, bias_tables, w_qkv, w_out, w_up, w_down, grad_out
):
    slots, width = features.shape[2:]
    heads = bias_tables.shape[2]
    hidden = w_up.shape[2]
    points = (slots, width)
    vmem = pl.BlockSpec(memory_space=pltpu.VMEM)
    hbm = pl.BlockSpec(memory_space=pl.ANY)
    dma = pltpu.SemaphoreType.DMA
    scratch = [
        pltpu.VMEM(points, BF16),
        pltpu.VMEM(points, BF16),
        pltpu.VMEM(w_qkv.shape, BF16),
        pltpu.VMEM(w_out.shape, BF16),
        pltpu.VMEM(w_up.shape, BF16),
        pltpu.VMEM(w_down.shape, BF16),
        pltpu.VMEM((8, slots), jnp.int32),
        pltpu.VMEM((3, 8, slots), jnp.int32),
    ]
    scratch += [pltpu.VMEM(points, BF16) for _ in range(7)]
    scratch += [
        pltpu.VMEM((3, heads, slots), F32),
        pltpu.VMEM((heads * 32, slots), F32),
        pltpu.VMEM((2, heads, slots, slots), F32),
        pltpu.VMEM((heads * 32, slots), F32),
        pltpu.VMEM((2, heads, slots, slots), BF16),
        pltpu.VMEM((2, slots, 3 * width), BF16),
        pltpu.VMEM((2, width, slots), BF16),
        pltpu.VMEM((2,) + points, F32),
        pltpu.VMEM((2,) + points, F32),
        pltpu.VMEM((2, slots, 1), F32),
        pltpu.VMEM((2, slots, 1), F32),
        pltpu.VMEM((2, slots, hidden), F32),
        pltpu.VMEM((2, slots, slots), BF16),
        pltpu.VMEM((2, 32, slots), BF16),
        pltpu.VMEM((slots, heads * slots), BF16),
        pltpu.VMEM((heads * slots, width), BF16),
        pltpu.VMEM((heads * slots, width), BF16),
        pltpu.VMEM((2 * heads, slots), F32),
        pltpu.VMEM((nx, 2 * heads, slots), F32),
        pltpu.VMEM((2 * heads, slots), F32),
        pltpu.VMEM((ny, 2 * heads, slots), F32),
        dma((10,)), dma((15,)), dma((15,)), dma((nx,)), dma((nx,)), dma((ny,)), dma((ny,)),
    ]
    return pl.pallas_call(
        partial(kernel, nx, ny),
        out_shape=(
            jax.ShapeDtypeStruct(features.shape, BF16),
            jax.ShapeDtypeStruct(features.shape, BF16),
            jax.ShapeDtypeStruct(bias_tables.shape, F32),
        ),
        in_specs=[hbm, vmem, vmem, vmem, vmem, hbm, hbm, hbm, hbm, hbm],
        out_specs=(vmem, vmem, vmem),
        scratch_shapes=scratch,
        compiler_params=pltpu.CompilerParams(
            collective_id=0, has_side_effects=True, vmem_limit_bytes=60 * 1024 * 1024
        ),
    )(features, occupancy, coords, norm_gains, bias_tables, w_qkv, w_out, w_up, w_down, grad_out)


def solution(mesh):
    spread = P("gx", "gy", None, None)
    return jax.shard_map(
        partial(on_device, mesh.shape["gx"], mesh.shape["gy"]),
        mesh=mesh,
        in_specs=(spread, P("gx", "gy", None), spread, P(), P(), P(), P(), P(), P(), spread),
        out_specs=(spread, spread, P()),
        check_vma=False,
    )
```

```python
from functools import partial

import jax
import jax.numpy as jnp
from jax import lax
from jax.experimental import pallas as pl
from jax.experimental.pallas import tpu as pltpu
from jax.sharding import PartitionSpec as P

EPSILON = 1e-05
GELU_SCALE = 0.7978845608028654
GELU_CUBE = 0.044715
VMEM_BYTES = 67_043_328
MESH = pl.DeviceIdType.MESH
F32 = jnp.float32
BF16 = jnp.bfloat16


def dot_nn(a, b):
    return jnp.dot(a, b, preferred_element_type=F32)


def dot_nt(a, b):
    return lax.dot_general(a, b, (((1,), (1,)), ((), ())), preferred_element_type=F32)


def norm_parts(values):
    mean_value = jnp.mean(values, axis=-1, keepdims=True)
    centred = values - mean_value
    variance = jnp.mean(centred * centred, axis=-1, keepdims=True)
    scale = lax.rsqrt(variance + EPSILON)
    return centred * scale, scale


def norm_pullback(cotangent, gain, unit, scale):
    inner = cotangent * gain
    first = jnp.mean(inner, axis=-1, keepdims=True)
    second = jnp.mean(inner * unit, axis=-1, keepdims=True)
    return scale * (inner - first - unit * second)


def split_two(values):
    high = values.astype(BF16)
    return high, (values - high.astype(F32)).astype(BF16)


def kernel(
    nx, ny,
    feat, occ_h, coords_h, gains_h, tables_h, wqkv, wout, wup, wdown, gout,
    out_points, grad_points, grad_tables,
    occ, coords, gains, tables,
    x_v, g_v, wqkv_v, wout_v, wup_v, wdown_v,
    meta, meta_recv, g_roll, first, rolled, second, back, grad_mid, grad_first,
    table_pad, band, left_bias, diag, probs, proj, keys_t, unit_one, unit_two,
    rstd_one, rstd_two, gelu_in, expanded_v, cot_wide_v, onehot_s, onehot_t, score_cot, cot_pair,
    q_stack, mix_stack,
    t_send, t_recv_x, t_mid, t_recv_y,
    load_sem, send_sem, recv_sem, tx_send, tx_recv, ty_send, ty_recv,
):
    slots, width = x_v.shape
    quarter = slots // 4
    heads = tables.shape[2]
    span = tables.shape[3]
    cells = (span + 1) // 2
    half = cells // 2
    head_size = width // heads
    scale = head_size ** -0.5
    i = lax.axis_index("gx")
    j = lax.axis_index("gy")
    up_i, down_i = lax.rem(i + 1, nx), lax.rem(i + nx - 1, nx)
    up_j, down_j = lax.rem(j + 1, ny), lax.rem(j + ny - 1, ny)

    pairs = [(feat.at[0, 0], x_v)]
    for k in range(2):
        pairs += [
            (wqkv.at[k], wqkv_v.at[k]),
            (wout.at[k], wout_v.at[k]),
            (wup.at[k], wup_v.at[k]),
            (wdown.at[k], wdown_v.at[k]),
        ]
    pairs.append((gout.at[0, 0], g_v))
    pairs += [(occ_h, occ), (coords_h, coords), (gains_h, gains), (tables_h, tables)]
    loads = [pltpu.make_async_copy(a, b, load_sem.at[n]) for n, (a, b) in enumerate(pairs)]
    for n in (10, 11, 12, 13, *range(10)):
        loads[n].start()

    barrier = pltpu.get_barrier_semaphore()
    for step in range(1, nx):
        pl.semaphore_signal(barrier, 1, device_id=(lax.rem(i + step, nx), j), device_id_type=MESH)
    for step in range(1, ny):
        pl.semaphore_signal(barrier, 1, device_id=(i, lax.rem(j + step, ny)), device_id_type=MESH)
    pl.semaphore_signal(barrier, 1, device_id=(up_i, up_j), device_id_type=MESH)
    pl.semaphore_signal(barrier, 1, device_id=(down_i, down_j), device_id_type=MESH)

    def remote(source, target, place, device):
        return pltpu.make_async_remote_copy(
            src_ref=source, dst_ref=target, send_sem=send_sem.at[place],
            recv_sem=recv_sem.at[place], device_id=device, device_id_type=MESH,
        )

    def rows(number):
        return pl.ds(number * quarter, quarter)

    def roll_forward(source, target, base):
        copies = [
            remote(source.at[rows(0)], target.at[rows(3)], base, (down_i, down_j)),
            remote(source.at[rows(1)], target.at[rows(2)], base + 1, (down_i, j)),
            remote(source.at[rows(2)], target.at[rows(1)], base + 2, (i, down_j)),
        ]
        for copy in copies:
            copy.start()
        target[rows(0)] = source[rows(3)]
        return copies

    def roll_backward(source, target, base):
        copies = [
            remote(source.at[rows(3)], target.at[rows(0)], base, (up_i, up_j)),
            remote(source.at[rows(2)], target.at[rows(1)], base + 1, (up_i, j)),
            remote(source.at[rows(1)], target.at[rows(2)], base + 2, (i, up_j)),
        ]
        for copy in copies:
            copy.start()
        target[rows(3)] = source[rows(0)]
        return copies

    lane = lax.broadcasted_iota(jnp.int32, (heads, slots), 1)
    lane_row = lax.broadcasted_iota(jnp.int32, (1, slots), 1)
    channel = lax.broadcasted_iota(jnp.int32, (1, width), 1)
    head_masks = [
        ((channel >= h * head_size) & (channel < (h + 1) * head_size)).astype(F32).astype(BF16)
        for h in range(heads)
    ]
    pad_rows = 32

    def prepare_bias(k, occupied_row, coord_rows):
        cell = lax.broadcasted_iota(jnp.int32, (cells, slots), 0)
        blocks = [(jnp.broadcast_to(c, (cells, slots)) == cell).astype(F32) for c in coord_rows]
        empty = jnp.zeros((cells, slots), F32)
        first_row = cell == 0
        mask_block = jnp.where(
            first_row, jnp.broadcast_to(occupied_row.astype(F32) - 1.0, (cells, slots)), 0.0
        )
        one_block = jnp.where(first_row, 1.0, 0.0)
        rest = jnp.zeros((slots - 2 * pad_rows, slots), F32)
        right = jnp.concatenate(
            blocks + [one_block] + blocks + [empty, rest], axis=0
        ).astype(BF16)
        left = jnp.concatenate(blocks + [mask_block, empty, empty, empty, empty, rest], axis=0)
        left_t = jnp.transpose(left)
        onehot_s[k] = left_t.astype(BF16)
        onehot_t[k] = jnp.concatenate(blocks + [empty], axis=0).astype(BF16)
        table_pad[...] = jnp.zeros_like(table_pad)
        for e in range(3):
            table_pad[e, :, 0:span] = tables[k, e]
        mask_row = jnp.where(lane == 3 * cells, 1e30, 0.0)
        for u in range(cells):
            row = mask_row if u == 0 else jnp.zeros_like(mask_row)
            band[pl.ds(3 * cells + u, heads, stride=pad_rows), :] = row
        for e in range(3):
            padded = table_pad[e]
            inside = (lane >= e * cells) & (lane < (e + 1) * cells)
            for u in range(cells):
                shift = (e * cells + u - (cells - 1)) % slots
                moved = pltpu.roll(padded, shift, 1) if shift else padded
                tile = jnp.where(inside, moved, 0.0)
                high = tile.astype(BF16).astype(F32)
                tile = high + pltpu.roll(tile - high, pad_rows, 1)
                band[pl.ds(e * cells + u, heads, stride=pad_rows), :] = tile
        left_hot = onehot_s[k][:, 0:pad_rows]
        banded = jnp.concatenate(
            [band[h * pad_rows:(h + 1) * pad_rows, :] for h in range(heads)], axis=1
        ).astype(BF16)
        factors = dot_nn(left_hot, banded).astype(BF16)
        factors = jnp.concatenate(
            [factors[:, h * slots:(h + 1) * slots] for h in range(heads)], axis=0
        )
        left_bias[k] = dot_nn(factors, right)
        return left_t[:, 3 * cells:3 * cells + 1] + 1.0

    def stacked(values):
        return jnp.concatenate([values * head_masks[h] for h in range(heads)], axis=0)

    def attention_head(k, hidden):
        unit, rstd = norm_parts(hidden)
        unit_one[k] = unit
        rstd_one[k] = rstd
        normed = (unit * gains[k, 0:1]).astype(BF16)
        loads[1 + 4 * k].wait()
        projected = dot_nn(normed, wqkv_v[k])
        proj[k] = projected.astype(BF16)
        keys_t[k] = jnp.transpose(projected[:, width:2 * width]).astype(BF16)
        return jnp.transpose(projected[:, 2 * width:]).astype(BF16)

    def attention_part(k, hidden, values_t):
        queries = proj[k, :, 0:width]
        keys = proj[k, :, width:2 * width]
        scores_all = dot_nt(stacked(keys), queries)
        pieces = []
        for h in range(heads):
            here = slice(h * slots, (h + 1) * slots)
            scores = scores_all[here] * scale + left_bias[k, here]
            top = jnp.max(scores, axis=0, keepdims=True)
            powers = jnp.exp(scores - top)
            weights = (powers * (1.0 / jnp.sum(powers, axis=0, keepdims=True))).astype(BF16)
            probs[k, here] = weights
            pieces.append(dot_nn(values_t[h * head_size:(h + 1) * head_size], weights))
        mixed = jnp.transpose(jnp.concatenate(pieces, axis=0)).astype(BF16)
        loads[2 + 4 * k].wait()
        return hidden + dot_nn(mixed, wout_v[k])

    hidden_width = wup_v.shape[2]
    chunk = 2 * slots
    chunks = [pl.ds(start, chunk) for start in range(0, hidden_width, chunk)]

    def feed_part(k, middle, with_slope):
        unit, rstd = norm_parts(middle)
        unit_two[k] = unit
        rstd_two[k] = rstd
        normed = (unit * gains[k, 1:2]).astype(BF16)
        loads[3 + 4 * k].wait()
        for cut in chunks:
            wide = dot_nn(normed, wup_v[k, :, cut])
            square = wide * wide
            inner = jnp.tanh(wide * (GELU_SCALE + (GELU_SCALE * GELU_CUBE) * square))
            grown = 0.5 * (1.0 + inner)
            expanded_v[k, :, cut] = (wide * grown).astype(BF16)
            if with_slope:
                gelu_in[k, :, cut] = grown + wide * (0.5 * (1.0 - inner * inner)) * (
                    GELU_SCALE + (3.0 * GELU_SCALE * GELU_CUBE) * square
                )
            else:
                gelu_in[k, :, cut] = wide

    def feed_out(k, middle):
        loads[4 + 4 * k].wait()
        return (middle + dot_nn(expanded_v[k], wdown_v[k])).astype(BF16)

    def gelu_slope(k):
        for cut in chunks:
            wide = gelu_in[k, :, cut]
            square = wide * wide
            inner = jnp.tanh(wide * (GELU_SCALE + (GELU_SCALE * GELU_CUBE) * square))
            gelu_in[k, :, cut] = 0.5 * (1.0 + inner) + wide * (0.5 * (1.0 - inner * inner)) * (
                GELU_SCALE + (3.0 * GELU_SCALE * GELU_CUBE) * square
            )

    def pull_wide(k, cotangent):
        for cut in chunks:
            cot_wide_v[k, :, cut] = dot_nt(cotangent, wdown_v[k, cut, :]).astype(BF16)

    def pull_scores(k, cotangent):
        for cut in chunks:
            cot_wide_v[k, :, cut] = (
                cot_wide_v[k, :, cut].astype(F32) * gelu_in[k, :, cut]
            ).astype(BF16)
        cot_normed = dot_nt(cot_wide_v[k], wup_v[k]).astype(BF16).astype(F32)
        cot_middle = cotangent.astype(F32) + norm_pullback(
            cot_normed, gains[k, 1:2], unit_two[k], rstd_two[k]
        )
        cot_mixed = dot_nt(cot_middle.astype(BF16), wout_v[k]).astype(BF16)
        mix_stack[...] = stacked(cot_mixed)
        cot_all = dot_nt(stacked(proj[k, :, 2 * width:]), cot_mixed)
        for h in range(heads):
            here = slice(h * slots, (h + 1) * slots)
            cot_probs = cot_all[here].astype(BF16).astype(F32)
            weights = probs[k, here].astype(F32)
            product = weights * cot_probs
            total = jnp.sum(product, axis=0, keepdims=True)
            high, low = split_two(product - weights * total)
            cot_pair[here, 0:slots] = high
            cot_pair[here, slots:2 * slots] = low
        return cot_middle

    def table_sums(k):
        hot_twice = jnp.concatenate([onehot_s[k], onehot_s[k]], axis=0)
        hot_t_twice = jnp.concatenate([onehot_t[k], onehot_t[k]], axis=1)
        by_key = dot_nn(cot_pair[...], hot_twice)
        key_high, key_low = split_two(by_key)
        pair = jnp.concatenate(
            [
                jnp.concatenate(
                    [part[h * slots:(h + 1) * slots] for h in range(heads)], axis=1
                )
                for part in (key_high, key_low)
            ],
            axis=0,
        )
        pairs_sum = dot_nn(hot_t_twice, pair)
        for h in range(heads):
            diag[h * pad_rows:(h + 1) * pad_rows, :] = pairs_sum[:, h * slots:(h + 1) * slots]
        sums = []
        for e in range(3):
            inside = (lane >= e * cells) & (lane < (e + 1) * cells)
            for u in range(cells):
                tile = jnp.where(inside, diag[pl.ds(e * cells + u, heads, stride=pad_rows), :], 0.0)
                shift = e * cells + (cells - 1) - u
                sums.append(pltpu.roll(tile, shift, 1) if shift else tile)
        while len(sums) > 1:
            sums = [a + b for a, b in zip(sums[0::2], sums[1::2])] + (
                [sums[-1]] if len(sums) % 2 else []
            )
        t_send[k * heads:(k + 1) * heads, :] = sums[0]

    def pull_proj(k):
        pieces = []
        for h in range(heads):
            high = cot_pair[h * slots:(h + 1) * slots, 0:slots]
            score_cot[:, h * slots:(h + 1) * slots] = high
            pieces.append(dot_nn(keys_t[k, h * head_size:(h + 1) * head_size], high))
        q_stack[...] = stacked(proj[k, :, 0:width])
        cot_queries = (jnp.transpose(jnp.concatenate(pieces, axis=0)) * scale).astype(BF16)
        cot_keys = (dot_nn(score_cot[...], q_stack[...]) * scale).astype(BF16)
        probs_wide = jnp.concatenate(
            [probs[k, h * slots:(h + 1) * slots] for h in range(heads)], axis=1
        )
        cot_values = dot_nn(probs_wide, mix_stack[...]).astype(BF16)
        return jnp.concatenate([cot_queries, cot_keys, cot_values], axis=1)

    def pull_input(k, cot_proj, cot_middle):
        cot_normed = dot_nt(cot_proj, wqkv_v[k]).astype(BF16).astype(F32)
        return (
            cot_middle + norm_pullback(cot_normed, gains[k, 0:1], unit_one[k], rstd_one[k])
        ).astype(BF16)

    for n in (10, 11, 12, 13):
        loads[n].wait()
    meta[...] = jnp.zeros_like(meta)
    meta[0:1, :] = occ[0]
    for e in range(3):
        meta[e + 1:e + 2, :] = coords[0, e]
    loads[0].wait()
    hidden = x_v[...].astype(F32)
    values_t = attention_head(0, hidden)
    occupied = prepare_bias(0, occ[0], [coords[0, e] for e in range(3)])
    middle = attention_part(0, hidden, values_t)

    pl.semaphore_wait(barrier, nx + ny)
    meta_copies = [
        remote(meta, meta_recv.at[0], 0, (down_i, down_j)),
        remote(meta, meta_recv.at[1], 1, (down_i, j)),
        remote(meta, meta_recv.at[2], 2, (i, down_j)),
    ]
    for copy in meta_copies:
        copy.start()
    loads[9].wait()
    grad_copies = roll_forward(g_v, g_roll, 3)

    feed_part(0, middle, False)
    first[...] = feed_out(0, middle)
    first_copies = roll_forward(first, rolled, 6)

    for copy in meta_copies:
        copy.wait()
    own = pltpu.roll(meta[...], quarter, 1)
    from_y = pltpu.roll(meta_recv[2], slots - quarter, 1)
    from_x = pltpu.roll(meta_recv[1], quarter, 1)
    from_xy = pltpu.roll(meta_recv[0], slots - quarter, 1)
    moved = jnp.where(
        lane_row < quarter, own,
        jnp.where(lane_row < 2 * quarter, from_y, jnp.where(lane_row < 3 * quarter, from_x, from_xy)),
    )

    def wrapped(values):
        moved_on = values + half
        return jnp.where(moved_on >= cells, moved_on - cells, moved_on)

    shifted_occupied = prepare_bias(
        1, moved[0:1], [wrapped(moved[1:2]), wrapped(moved[2:3]), moved[3:4]]
    )
    gelu_slope(0)
    for copy in grad_copies:
        copy.wait()
    grad_in = (g_roll[...].astype(F32) * shifted_occupied).astype(BF16)
    loads[8].wait()
    pull_wide(1, grad_in)
    for copy in first_copies:
        copy.wait()
    hidden = rolled[...].astype(F32)
    middle = attention_part(1, hidden, attention_head(1, hidden))
    feed_part(1, middle, True)
    cot_middle = pull_scores(1, grad_in)
    grad_mid[...] = pull_input(1, pull_proj(1), cot_middle)
    mid_copies = roll_backward(grad_mid, grad_first, 12)
    second[...] = (middle + dot_nn(expanded_v[1], wdown_v[1])).astype(BF16)
    second_copies = roll_backward(second, back, 9)
    table_sums(1)
    for copy in mid_copies:
        copy.wait()

    def exchange(source, target, send, recv, me, count, device_of):
        copies = []
        for step in range(1, count):
            copies.append(
                pltpu.make_async_remote_copy(
                    src_ref=source, dst_ref=target.at[me], send_sem=send.at[step],
                    recv_sem=recv.at[step], device_id=device_of(lax.rem(me + step, count)),
                    device_id_type=MESH,
                )
            )
            copies[-1].start()
        target[me] = source[...]
        return copies

    cotangent = grad_first[...]
    pull_wide(0, cotangent)
    cot_middle = pull_scores(0, cotangent)
    table_sums(0)
    table_copies = exchange(t_send, t_recv_x, tx_send, tx_recv, i, nx, lambda other: (other, j))
    cot_proj = pull_proj(0)
    for copy in table_copies:
        copy.wait()
    total = t_recv_x[0]
    for n in range(1, nx):
        total = total + t_recv_x[n]
    t_mid[...] = total
    table_copies = exchange(t_mid, t_recv_y, ty_send, ty_recv, j, ny, lambda other: (i, other))
    grad_points[0, 0] = pull_input(0, cot_proj, cot_middle)
    for copy in second_copies:
        copy.wait()
    out_points[0, 0] = (back[...].astype(F32) * occupied).astype(BF16)
    for copy in table_copies:
        copy.wait()
    total = t_recv_y[0]
    for n in range(1, ny):
        total = total + t_recv_y[n]
    for k in range(2):
        for e in range(3):
            tile = total[k * heads:(k + 1) * heads]
            shift = (slots - 2 * cells * e) % slots
            tile = pltpu.roll(tile, shift, 1) if shift else tile
            grad_tables[k, e] = tile[:, 0:span]


def finish(points_in, grads_in, tables_in, points_out, grads_out, tables_out):
    points_out[...] = points_in[...]
    grads_out[...] = grads_in[...]
    tables_out[...] = tables_in[...]


def on_device(
    nx, ny, features, occupancy, coords, norm_gains, bias_tables, w_qkv, w_out, w_up, w_down, grad_out
):
    slots, width = features.shape[2:]
    coords = jnp.transpose(coords, (0, 2, 1, 3))
    heads = bias_tables.shape[2]
    hidden = w_up.shape[2]
    points = (slots, width)
    vmem = pl.BlockSpec(memory_space=pltpu.VMEM)
    hbm = pl.BlockSpec(memory_space=pltpu.HBM)
    dma = pltpu.SemaphoreType.DMA
    scratch = [
        pltpu.VMEM(occupancy.shape, jnp.int32),
        pltpu.VMEM(coords.shape, jnp.int32),
        pltpu.VMEM(norm_gains.shape, F32),
        pltpu.VMEM(bias_tables.shape, F32),
        pltpu.VMEM(points, BF16),
        pltpu.VMEM(points, BF16),
        pltpu.VMEM(w_qkv.shape, BF16),
        pltpu.VMEM(w_out.shape, BF16),
        pltpu.VMEM(w_up.shape, BF16),
        pltpu.VMEM(w_down.shape, BF16),
        pltpu.VMEM((8, slots), jnp.int32),
        pltpu.VMEM((3, 8, slots), jnp.int32),
    ]
    scratch += [pltpu.VMEM(points, BF16) for _ in range(7)]
    scratch += [
        pltpu.VMEM((3, heads, slots), F32),
        pltpu.VMEM((heads * 32, slots), F32),
        pltpu.VMEM((2, heads * slots, slots), F32),
        pltpu.VMEM((heads * 32, slots), F32),
        pltpu.VMEM((2, heads * slots, slots), BF16),
        pltpu.VMEM((2, slots, 3 * width), BF16),
        pltpu.VMEM((2, width, slots), BF16),
        pltpu.VMEM((2,) + points, F32),
        pltpu.VMEM((2,) + points, F32),
        pltpu.VMEM((2, slots, 1), F32),
        pltpu.VMEM((2, slots, 1), F32),
        pltpu.VMEM((2, slots, hidden), F32),
        pltpu.VMEM((2, slots, hidden), BF16),
        pltpu.VMEM((2, slots, hidden), BF16),
        pltpu.VMEM((2, slots, slots), BF16),
        pltpu.VMEM((2, 32, slots), BF16),
        pltpu.VMEM((slots, heads * slots), BF16),
        pltpu.VMEM((heads * slots, 2 * slots), BF16),
        pltpu.VMEM((heads * slots, width), BF16),
        pltpu.VMEM((heads * slots, width), BF16),
        pltpu.VMEM((2 * heads, slots), F32),
        pltpu.VMEM((nx, 2 * heads, slots), F32),
        pltpu.VMEM((2 * heads, slots), F32),
        pltpu.VMEM((ny, 2 * heads, slots), F32),
        dma((14,)), dma((15,)), dma((15,)), dma((nx,)), dma((nx,)), dma((ny,)), dma((ny,)),
    ]
    shapes = [(features.shape, BF16), (features.shape, BF16), (bias_tables.shape, F32)]
    padded_tables = 6 * 8 * slots * 4 * pl.cdiv(heads, 8)
    room = VMEM_BYTES - 4 * slots * width - padded_tables
    results = pl.pallas_call(
        partial(kernel, nx, ny),
        out_shape=[pltpu.VMEM(*shape) for shape in shapes],
        in_specs=[hbm] * 10,
        out_specs=[vmem] * 3,
        scratch_shapes=scratch,
        compiler_params=pltpu.CompilerParams(
            collective_id=0, has_side_effects=True, vmem_limit_bytes=room
        ),
    )(features, occupancy, coords, norm_gains, bias_tables, w_qkv, w_out, w_up, w_down, grad_out)
    return tuple(pl.pallas_call(
        finish,
        out_shape=[jax.ShapeDtypeStruct(*shape) for shape in shapes],
        in_specs=[vmem] * 3,
        out_specs=[vmem] * 3,
        compiler_params=pltpu.CompilerParams(vmem_limit_bytes=2 * 1024 * 1024),
    )(*results))


def solution(mesh):
    spread = P("gx", "gy", None, None)
    return jax.shard_map(
        partial(on_device, mesh.shape["gx"], mesh.shape["gy"]),
        mesh=mesh,
        in_specs=(spread, P("gx", "gy", None), spread, P(), P(), P(), P(), P(), P(), spread),
        out_specs=(spread, spread, P()),
        check_vma=False,
    )
```

```python
from functools import partial

import jax
import jax.numpy as jnp
from jax import lax
from jax.experimental import pallas as pl
from jax.experimental.pallas import tpu as pltpu
from jax.sharding import PartitionSpec as P

EPSILON = 1e-05
GELU_SCALE = 0.7978845608028654
GELU_CUBE = 0.044715
VMEM_BYTES = 67_043_328
MESH = pl.DeviceIdType.MESH
F32 = jnp.float32
BF16 = jnp.bfloat16


def dot_nn(a, b):
    return jnp.dot(a, b, preferred_element_type=F32)


def dot_nt(a, b):
    return lax.dot_general(a, b, (((1,), (1,)), ((), ())), preferred_element_type=F32)


def norm_parts(values):
    mean_value = jnp.mean(values, axis=-1, keepdims=True)
    centred = values - mean_value
    variance = jnp.mean(centred * centred, axis=-1, keepdims=True)
    scale = lax.rsqrt(variance + EPSILON)
    return centred * scale, scale


def norm_pullback(cotangent, gain, unit, scale):
    inner = cotangent * gain
    first = jnp.mean(inner, axis=-1, keepdims=True)
    second = jnp.mean(inner * unit, axis=-1, keepdims=True)
    return scale * (inner - first - unit * second)


def split_two(values):
    high = values.astype(BF16)
    return high, (values - high.astype(F32)).astype(BF16)


def kernel(
    nx, ny,
    feat, occ_h, coords_h, gains_h, tables_h, wqkv, wout, wup, wdown, gout,
    out_points, grad_points, grad_tables,
    occ, coords, gains, tables,
    x_v, g_v, wqkv_v, wout_v, wup_v, wdown_v,
    meta, meta_recv, g_roll, first, rolled, second, back, grad_mid, grad_first,
    table_pad, band, left_bias, diag, probs, proj, keys_t, unit_one, unit_two,
    rstd_one, rstd_two, gelu_in, expanded_v, cot_wide_v, onehot_s, onehot_t, cot_pair,
    q_stack, v_stack, mix_stack,
    t_send, t_recv_x, t_mid, t_recv_y,
    load_sem, send_sem, recv_sem, tx_send, tx_recv, ty_send, ty_recv,
):
    slots, width = x_v.shape
    quarter = slots // 4
    heads = tables.shape[2]
    span = tables.shape[3]
    cells = (span + 1) // 2
    half = cells // 2
    head_size = width // heads
    scale = head_size ** -0.5
    i = lax.axis_index("gx")
    j = lax.axis_index("gy")
    up_i, down_i = lax.rem(i + 1, nx), lax.rem(i + nx - 1, nx)
    up_j, down_j = lax.rem(j + 1, ny), lax.rem(j + ny - 1, ny)

    pairs = [(feat.at[0, 0], x_v)]
    for k in range(2):
        pairs += [
            (wqkv.at[k], wqkv_v.at[k]),
            (wout.at[k], wout_v.at[k]),
            (wup.at[k], wup_v.at[k]),
            (wdown.at[k], wdown_v.at[k]),
        ]
    pairs.append((gout.at[0, 0], g_v))
    pairs += [(occ_h, occ), (coords_h, coords), (gains_h, gains), (tables_h, tables)]
    loads = [pltpu.make_async_copy(a, b, load_sem.at[n]) for n, (a, b) in enumerate(pairs)]
    for n in (10, 11, 12, 13, *range(10)):
        loads[n].start()

    barrier = pltpu.get_barrier_semaphore()
    for step in range(1, nx):
        pl.semaphore_signal(barrier, 1, device_id=(lax.rem(i + step, nx), j), device_id_type=MESH)
    for step in range(1, ny):
        pl.semaphore_signal(barrier, 1, device_id=(i, lax.rem(j + step, ny)), device_id_type=MESH)
    pl.semaphore_signal(barrier, 1, device_id=(up_i, up_j), device_id_type=MESH)
    pl.semaphore_signal(barrier, 1, device_id=(down_i, down_j), device_id_type=MESH)

    def remote(source, target, place, device):
        return pltpu.make_async_remote_copy(
            src_ref=source, dst_ref=target, send_sem=send_sem.at[place],
            recv_sem=recv_sem.at[place], device_id=device, device_id_type=MESH,
        )

    def rows(number):
        return pl.ds(number * quarter, quarter)

    def roll_forward(source, target, base):
        copies = [
            remote(source.at[rows(0)], target.at[rows(3)], base, (down_i, down_j)),
            remote(source.at[rows(1)], target.at[rows(2)], base + 1, (down_i, j)),
            remote(source.at[rows(2)], target.at[rows(1)], base + 2, (i, down_j)),
        ]
        for copy in copies:
            copy.start()
        target[rows(0)] = source[rows(3)]
        return copies

    def roll_backward(source, target, base):
        copies = [
            remote(source.at[rows(3)], target.at[rows(0)], base, (up_i, up_j)),
            remote(source.at[rows(2)], target.at[rows(1)], base + 1, (up_i, j)),
            remote(source.at[rows(1)], target.at[rows(2)], base + 2, (i, up_j)),
        ]
        for copy in copies:
            copy.start()
        target[rows(3)] = source[rows(0)]
        return copies

    lane = lax.broadcasted_iota(jnp.int32, (heads, slots), 1)
    lane_row = lax.broadcasted_iota(jnp.int32, (1, slots), 1)
    channel = lax.broadcasted_iota(jnp.int32, (1, width), 1)
    head_masks = [
        ((channel >= h * head_size) & (channel < (h + 1) * head_size)).astype(F32).astype(BF16)
        for h in range(heads)
    ]
    pad_rows = 32

    def prepare_bias(k, occupied_row, coord_rows):
        cell = lax.broadcasted_iota(jnp.int32, (cells, slots), 0)
        blocks = [(jnp.broadcast_to(c, (cells, slots)) == cell).astype(F32) for c in coord_rows]
        empty = jnp.zeros((cells, slots), F32)
        first_row = cell == 0
        mask_block = jnp.where(
            first_row, jnp.broadcast_to(occupied_row.astype(F32) - 1.0, (cells, slots)), 0.0
        )
        one_block = jnp.where(first_row, 1.0, 0.0)
        rest = jnp.zeros((slots - 2 * pad_rows, slots), F32)
        right = jnp.concatenate(
            blocks + [one_block] + blocks + [empty, rest], axis=0
        ).astype(BF16)
        left = jnp.concatenate(blocks + [mask_block, empty, empty, empty, empty, rest], axis=0)
        left_t = jnp.transpose(left)
        onehot_s[k] = left_t.astype(BF16)
        onehot_t[k] = jnp.concatenate(blocks + [empty], axis=0).astype(BF16)
        table_pad[...] = jnp.zeros_like(table_pad)
        for e in range(3):
            table_pad[e, :, 0:span] = tables[k, e]
        mask_row = jnp.where(lane == 3 * cells, 1e30, 0.0)
        for u in range(cells):
            row = mask_row if u == 0 else jnp.zeros_like(mask_row)
            band[pl.ds(3 * cells + u, heads, stride=pad_rows), :] = row
        for e in range(3):
            padded = table_pad[e]
            inside = (lane >= e * cells) & (lane < (e + 1) * cells)
            for u in range(cells):
                shift = (e * cells + u - (cells - 1)) % slots
                moved = pltpu.roll(padded, shift, 1) if shift else padded
                tile = jnp.where(inside, moved, 0.0)
                high = tile.astype(BF16).astype(F32)
                tile = high + pltpu.roll(tile - high, pad_rows, 1)
                band[pl.ds(e * cells + u, heads, stride=pad_rows), :] = tile
        left_hot = onehot_s[k][:, 0:pad_rows]
        banded = jnp.concatenate(
            [band[h * pad_rows:(h + 1) * pad_rows, :] for h in range(heads)], axis=1
        ).astype(BF16)
        factors = dot_nn(left_hot, banded).astype(BF16)
        factors = jnp.concatenate(
            [factors[:, h * slots:(h + 1) * slots] for h in range(heads)], axis=0
        )
        left_bias[k] = dot_nn(factors, right)
        return left_t[:, 3 * cells:3 * cells + 1] + 1.0

    def stacked(values):
        return jnp.concatenate([values * head_masks[h] for h in range(heads)], axis=0)

    def attention_head(k, hidden):
        unit, rstd = norm_parts(hidden)
        unit_one[k] = unit
        rstd_one[k] = rstd
        normed = (unit * gains[k, 0:1]).astype(BF16)
        loads[1 + 4 * k].wait()
        projected = dot_nn(normed, wqkv_v[k])
        proj[k] = projected.astype(BF16)
        keys_t[k] = jnp.transpose(projected[:, width:2 * width]).astype(BF16)
        return jnp.transpose(projected[:, 2 * width:]).astype(BF16)

    def attention_part(k, hidden, values_t):
        queries = proj[k, :, 0:width]
        keys = proj[k, :, width:2 * width]
        scores_all = dot_nt(stacked(keys), queries)
        pieces = []
        for h in range(heads):
            here = slice(h * slots, (h + 1) * slots)
            scores = scores_all[here] * scale + left_bias[k, here]
            top = jnp.max(scores, axis=0, keepdims=True)
            powers = jnp.exp(scores - top)
            weights = (powers * (1.0 / jnp.sum(powers, axis=0, keepdims=True))).astype(BF16)
            probs[k, here] = weights
            pieces.append(dot_nn(values_t[h * head_size:(h + 1) * head_size], weights))
        mixed = jnp.transpose(jnp.concatenate(pieces, axis=0)).astype(BF16)
        loads[2 + 4 * k].wait()
        return hidden + dot_nn(mixed, wout_v[k])

    hidden_width = wup_v.shape[2]
    chunk = 2 * slots
    chunks = [pl.ds(start, chunk) for start in range(0, hidden_width, chunk)]

    def feed_part(k, middle, with_slope):
        unit, rstd = norm_parts(middle)
        unit_two[k] = unit
        rstd_two[k] = rstd
        normed = (unit * gains[k, 1:2]).astype(BF16)
        loads[3 + 4 * k].wait()
        for cut in chunks:
            wide = dot_nn(normed, wup_v[k, :, cut])
            square = wide * wide
            inner = jnp.tanh(wide * (GELU_SCALE + (GELU_SCALE * GELU_CUBE) * square))
            grown = 0.5 * (1.0 + inner)
            expanded_v[k, :, cut] = (wide * grown).astype(BF16)
            if with_slope:
                gelu_in[k, :, cut] = grown + wide * (0.5 * (1.0 - inner * inner)) * (
                    GELU_SCALE + (3.0 * GELU_SCALE * GELU_CUBE) * square
                )
            else:
                gelu_in[k, :, cut] = wide

    def feed_out(k, middle):
        loads[4 + 4 * k].wait()
        return (middle + dot_nn(expanded_v[k], wdown_v[k])).astype(BF16)

    def gelu_slope(k):
        for cut in chunks:
            wide = gelu_in[k, :, cut]
            square = wide * wide
            inner = jnp.tanh(wide * (GELU_SCALE + (GELU_SCALE * GELU_CUBE) * square))
            gelu_in[k, :, cut] = 0.5 * (1.0 + inner) + wide * (0.5 * (1.0 - inner * inner)) * (
                GELU_SCALE + (3.0 * GELU_SCALE * GELU_CUBE) * square
            )

    def stack_parts(k):
        q_stack[k] = stacked(proj[k, :, 0:width])
        v_stack[k] = stacked(proj[k, :, 2 * width:])

    def pull_wide(k, cotangent):
        for cut in chunks:
            cot_wide_v[k, :, cut] = dot_nt(cotangent, wdown_v[k, cut, :]).astype(BF16)

    def pull_scores(k, cotangent):
        for cut in chunks:
            cot_wide_v[k, :, cut] = (
                cot_wide_v[k, :, cut].astype(F32) * gelu_in[k, :, cut]
            ).astype(BF16)
        cot_normed = dot_nt(cot_wide_v[k], wup_v[k]).astype(BF16).astype(F32)
        cot_middle = cotangent.astype(F32) + norm_pullback(
            cot_normed, gains[k, 1:2], unit_two[k], rstd_two[k]
        )
        cot_mixed = dot_nt(cot_middle.astype(BF16), wout_v[k]).astype(BF16)
        mix_stack[...] = stacked(cot_mixed)
        cot_all = dot_nt(v_stack[k], cot_mixed)
        for h in range(heads):
            here = slice(h * slots, (h + 1) * slots)
            cot_probs = cot_all[here].astype(BF16).astype(F32)
            weights = probs[k, here].astype(F32)
            product = weights * cot_probs
            total = jnp.sum(product, axis=0, keepdims=True)
            high, low = split_two(product - weights * total)
            cot_pair[0:slots, here] = high
            cot_pair[slots:2 * slots, here] = low
        return cot_middle

    def table_sums(k):
        hot_twice = jnp.concatenate([onehot_s[k], onehot_s[k]], axis=0)
        hot_t_twice = jnp.concatenate([onehot_t[k], onehot_t[k]], axis=1)
        by_cell = dot_nn(hot_t_twice, cot_pair[...])
        by_cell = jnp.concatenate(
            [by_cell[:, h * slots:(h + 1) * slots] for h in range(heads)], axis=0
        )
        diag[...] = dot_nn(jnp.concatenate(split_two(by_cell), axis=1), hot_twice)
        sums = []
        for e in range(3):
            inside = (lane >= e * cells) & (lane < (e + 1) * cells)
            for u in range(cells):
                tile = jnp.where(inside, diag[pl.ds(e * cells + u, heads, stride=pad_rows), :], 0.0)
                shift = e * cells + (cells - 1) - u
                sums.append(pltpu.roll(tile, shift, 1) if shift else tile)
        while len(sums) > 1:
            sums = [a + b for a, b in zip(sums[0::2], sums[1::2])] + (
                [sums[-1]] if len(sums) % 2 else []
            )
        t_send[k * heads:(k + 1) * heads, :] = sums[0]

    def pull_proj(k):
        pieces = []
        for h in range(heads):
            high = cot_pair[0:slots, h * slots:(h + 1) * slots]
            pieces.append(dot_nn(keys_t[k, h * head_size:(h + 1) * head_size], high))
        cot_queries = (jnp.transpose(jnp.concatenate(pieces, axis=0)) * scale).astype(BF16)
        cot_keys = (dot_nn(cot_pair[0:slots, :], q_stack[k]) * scale).astype(BF16)
        probs_wide = jnp.concatenate(
            [probs[k, h * slots:(h + 1) * slots] for h in range(heads)], axis=1
        )
        cot_values = dot_nn(probs_wide, mix_stack[...]).astype(BF16)
        return jnp.concatenate([cot_queries, cot_keys, cot_values], axis=1)

    def pull_input(k, cot_proj, cot_middle):
        cot_normed = dot_nt(cot_proj, wqkv_v[k]).astype(BF16).astype(F32)
        return (
            cot_middle + norm_pullback(cot_normed, gains[k, 0:1], unit_one[k], rstd_one[k])
        ).astype(BF16)

    for n in (10, 11, 12, 13):
        loads[n].wait()
    meta[...] = jnp.zeros_like(meta)
    meta[0:1, :] = occ[0]
    for e in range(3):
        meta[e + 1:e + 2, :] = coords[0, e]
    occupied = prepare_bias(0, occ[0], [coords[0, e] for e in range(3)])
    loads[0].wait()
    hidden = x_v[...].astype(F32)
    values_t = attention_head(0, hidden)
    middle = attention_part(0, hidden, values_t)

    pl.semaphore_wait(barrier, nx + ny)
    meta_copies = [
        remote(meta, meta_recv.at[0], 0, (down_i, down_j)),
        remote(meta, meta_recv.at[1], 1, (down_i, j)),
        remote(meta, meta_recv.at[2], 2, (i, down_j)),
    ]
    for copy in meta_copies:
        copy.start()
    loads[9].wait()
    grad_copies = roll_forward(g_v, g_roll, 3)

    feed_part(0, middle, False)
    first[...] = feed_out(0, middle)
    first_copies = roll_forward(first, rolled, 6)

    for copy in meta_copies:
        copy.wait()
    own = pltpu.roll(meta[...], quarter, 1)
    from_y = pltpu.roll(meta_recv[2], slots - quarter, 1)
    from_x = pltpu.roll(meta_recv[1], quarter, 1)
    from_xy = pltpu.roll(meta_recv[0], slots - quarter, 1)
    moved = jnp.where(
        lane_row < quarter, own,
        jnp.where(lane_row < 2 * quarter, from_y, jnp.where(lane_row < 3 * quarter, from_x, from_xy)),
    )

    def wrapped(values):
        moved_on = values + half
        return jnp.where(moved_on >= cells, moved_on - cells, moved_on)

    shifted_occupied = prepare_bias(
        1, moved[0:1], [wrapped(moved[1:2]), wrapped(moved[2:3]), moved[3:4]]
    )
    gelu_slope(0)
    for copy in grad_copies:
        copy.wait()
    grad_in = (g_roll[...].astype(F32) * shifted_occupied).astype(BF16)
    loads[8].wait()
    pull_wide(1, grad_in)
    for copy in first_copies:
        copy.wait()
    hidden = rolled[...].astype(F32)
    middle = attention_part(1, hidden, attention_head(1, hidden))
    feed_part(1, middle, True)
    stack_parts(1)
    cot_middle = pull_scores(1, grad_in)
    grad_mid[...] = pull_input(1, pull_proj(1), cot_middle)
    mid_copies = roll_backward(grad_mid, grad_first, 12)
    second[...] = (middle + dot_nn(expanded_v[1], wdown_v[1])).astype(BF16)
    second_copies = roll_backward(second, back, 9)
    table_sums(1)
    stack_parts(0)
    for copy in mid_copies:
        copy.wait()

    def exchange(source, target, send, recv, me, count, device_of):
        copies = []
        for step in range(1, count):
            copies.append(
                pltpu.make_async_remote_copy(
                    src_ref=source, dst_ref=target.at[me], send_sem=send.at[step],
                    recv_sem=recv.at[step], device_id=device_of(lax.rem(me + step, count)),
                    device_id_type=MESH,
                )
            )
            copies[-1].start()
        target[me] = source[...]
        return copies

    cotangent = grad_first[...]
    pull_wide(0, cotangent)
    cot_middle = pull_scores(0, cotangent)
    table_sums(0)
    table_copies = exchange(t_send, t_recv_y, ty_send, ty_recv, j, ny, lambda other: (i, other))
    cot_proj = pull_proj(0)
    grad_points[0, 0] = pull_input(0, cot_proj, cot_middle)
    for copy in second_copies:
        copy.wait()
    out_points[0, 0] = (back[...].astype(F32) * occupied).astype(BF16)
    for copy in table_copies:
        copy.wait()
    total = t_recv_y[0]
    for n in range(1, ny):
        total = total + t_recv_y[n]
    t_mid[...] = total
    for copy in exchange(t_mid, t_recv_x, tx_send, tx_recv, i, nx, lambda other: (other, j)):
        copy.wait()
    total = t_recv_x[0]
    for n in range(1, nx):
        total = total + t_recv_x[n]
    for k in range(2):
        for e in range(3):
            tile = total[k * heads:(k + 1) * heads]
            shift = (slots - 2 * cells * e) % slots
            tile = pltpu.roll(tile, shift, 1) if shift else tile
            grad_tables[k, e] = tile[:, 0:span]


def finish(points_in, grads_in, tables_in, points_out, grads_out, tables_out):
    points_out[...] = points_in[...]
    grads_out[...] = grads_in[...]
    tables_out[...] = tables_in[...]


def on_device(
    nx, ny, features, occupancy, coords, norm_gains, bias_tables, w_qkv, w_out, w_up, w_down, grad_out
):
    slots, width = features.shape[2:]
    coords = jnp.transpose(coords, (0, 2, 1, 3))
    heads = bias_tables.shape[2]
    hidden = w_up.shape[2]
    points = (slots, width)
    vmem = pl.BlockSpec(memory_space=pltpu.VMEM)
    hbm = pl.BlockSpec(memory_space=pltpu.HBM)
    dma = pltpu.SemaphoreType.DMA
    scratch = [
        pltpu.VMEM(occupancy.shape, jnp.int32),
        pltpu.VMEM(coords.shape, jnp.int32),
        pltpu.VMEM(norm_gains.shape, F32),
        pltpu.VMEM(bias_tables.shape, F32),
        pltpu.VMEM(points, BF16),
        pltpu.VMEM(points, BF16),
        pltpu.VMEM(w_qkv.shape, BF16),
        pltpu.VMEM(w_out.shape, BF16),
        pltpu.VMEM(w_up.shape, BF16),
        pltpu.VMEM(w_down.shape, BF16),
        pltpu.VMEM((8, slots), jnp.int32),
        pltpu.VMEM((3, 8, slots), jnp.int32),
    ]
    scratch += [pltpu.VMEM(points, BF16) for _ in range(7)]
    scratch += [
        pltpu.VMEM((3, heads, slots), F32),
        pltpu.VMEM((heads * 32, slots), F32),
        pltpu.VMEM((2, heads * slots, slots), F32),
        pltpu.VMEM((heads * 32, slots), F32),
        pltpu.VMEM((2, heads * slots, slots), BF16),
        pltpu.VMEM((2, slots, 3 * width), BF16),
        pltpu.VMEM((2, width, slots), BF16),
        pltpu.VMEM((2,) + points, F32),
        pltpu.VMEM((2,) + points, F32),
        pltpu.VMEM((2, slots, 1), F32),
        pltpu.VMEM((2, slots, 1), F32),
        pltpu.VMEM((2, slots, hidden), F32),
        pltpu.VMEM((2, slots, hidden), BF16),
        pltpu.VMEM((2, slots, hidden), BF16),
        pltpu.VMEM((2, slots, slots), BF16),
        pltpu.VMEM((2, 32, slots), BF16),
        pltpu.VMEM((2 * slots, heads * slots), BF16),
        pltpu.VMEM((2, heads * slots, width), BF16),
        pltpu.VMEM((2, heads * slots, width), BF16),
        pltpu.VMEM((heads * slots, width), BF16),
        pltpu.VMEM((2 * heads, slots), F32),
        pltpu.VMEM((nx, 2 * heads, slots), F32),
        pltpu.VMEM((2 * heads, slots), F32),
        pltpu.VMEM((ny, 2 * heads, slots), F32),
        dma((14,)), dma((15,)), dma((15,)), dma((nx,)), dma((nx,)), dma((ny,)), dma((ny,)),
    ]
    shapes = [(features.shape, BF16), (features.shape, BF16), (bias_tables.shape, F32)]
    padded_tables = 6 * 8 * slots * 4 * pl.cdiv(heads, 8)
    room = VMEM_BYTES - 4 * slots * width - padded_tables
    results = pl.pallas_call(
        partial(kernel, nx, ny),
        out_shape=[pltpu.VMEM(*shape) for shape in shapes],
        in_specs=[hbm] * 10,
        out_specs=[vmem] * 3,
        scratch_shapes=scratch,
        compiler_params=pltpu.CompilerParams(
            collective_id=0, has_side_effects=True, vmem_limit_bytes=room
        ),
    )(features, occupancy, coords, norm_gains, bias_tables, w_qkv, w_out, w_up, w_down, grad_out)
    return tuple(pl.pallas_call(
        finish,
        out_shape=[jax.ShapeDtypeStruct(*shape) for shape in shapes],
        in_specs=[vmem] * 3,
        out_specs=[vmem] * 3,
        compiler_params=pltpu.CompilerParams(vmem_limit_bytes=2 * 1024 * 1024),
    )(*results))


def solution(mesh):
    spread = P("gx", "gy", None, None)
    return jax.shard_map(
        partial(on_device, mesh.shape["gx"], mesh.shape["gy"]),
        mesh=mesh,
        in_specs=(spread, P("gx", "gy", None), spread, P(), P(), P(), P(), P(), P(), spread),
        out_specs=(spread, spread, P()),
        check_vma=False,
    )
```

```python
from functools import partial

import jax
import jax.numpy as jnp
from jax import lax
from jax.experimental import pallas as pl
from jax.experimental.pallas import tpu as pltpu
from jax.sharding import PartitionSpec as P

EPSILON = 1e-05
GELU_SCALE = 0.7978845608028654
GELU_CUBE = 0.044715
VMEM_BYTES = 67_043_328
MESH = pl.DeviceIdType.MESH
F32 = jnp.float32
BF16 = jnp.bfloat16


def dot_nn(a, b):
    return jnp.dot(a, b, preferred_element_type=F32)


def dot_nt(a, b):
    return lax.dot_general(a, b, (((1,), (1,)), ((), ())), preferred_element_type=F32)


def norm_parts(values):
    mean_value = jnp.mean(values, axis=-1, keepdims=True)
    centred = values - mean_value
    variance = jnp.mean(centred * centred, axis=-1, keepdims=True)
    scale = lax.rsqrt(variance + EPSILON)
    return centred * scale, scale


def norm_pullback(cotangent, gain, unit, scale):
    inner = cotangent * gain
    first = jnp.mean(inner, axis=-1, keepdims=True)
    second = jnp.mean(inner * unit, axis=-1, keepdims=True)
    return scale * (inner - first - unit * second)


def split_two(values):
    high = values.astype(BF16)
    return high, (values - high.astype(F32)).astype(BF16)


def kernel(
    nx, ny,
    feat, occ_h, coords_h, gains_h, tables_h, wqkv, wout, wup, wdown, gout,
    out_points, grad_points, grad_tables,
    occ, coords, gains, tables,
    x_v, g_v, wqkv_v, wout_v, wup_v, wdown_v,
    meta, meta_recv, g_roll, first, rolled, second, back, grad_mid, grad_first,
    table_pad, band, left_bias, diag, probs, proj, keys_t, unit_one, unit_two,
    rstd_one, rstd_two, gelu_in, expanded_v, cot_wide_v, onehot_s, onehot_t, cot_pair,
    q_stack, v_stack, mix_stack,
    t_send, t_recv_x, t_mid, t_recv_y,
    load_sem, send_sem, recv_sem, tx_send, tx_recv, ty_send, ty_recv,
):
    slots, width = x_v.shape
    quarter = slots // 4
    heads = tables.shape[2]
    span = tables.shape[3]
    cells = (span + 1) // 2
    half = cells // 2
    head_size = width // heads
    scale = head_size ** -0.5
    i = lax.axis_index("gx")
    j = lax.axis_index("gy")
    up_i, down_i = lax.rem(i + 1, nx), lax.rem(i + nx - 1, nx)
    up_j, down_j = lax.rem(j + 1, ny), lax.rem(j + ny - 1, ny)

    pairs = [(feat.at[0, 0], x_v)]
    for k in range(2):
        pairs += [
            (wqkv.at[k], wqkv_v.at[k]),
            (wout.at[k], wout_v.at[k]),
            (wup.at[k], wup_v.at[k]),
            (wdown.at[k], wdown_v.at[k]),
        ]
    pairs.append((gout.at[0, 0], g_v))
    pairs += [(occ_h, occ), (coords_h, coords), (gains_h, gains), (tables_h, tables)]
    loads = [pltpu.make_async_copy(a, b, load_sem.at[n]) for n, (a, b) in enumerate(pairs)]
    for n in (10, 11, 12, 13, *range(10)):
        loads[n].start()

    barrier = pltpu.get_barrier_semaphore()
    for step in range(1, nx):
        pl.semaphore_signal(barrier, 1, device_id=(lax.rem(i + step, nx), j), device_id_type=MESH)
    for step in range(1, ny):
        pl.semaphore_signal(barrier, 1, device_id=(i, lax.rem(j + step, ny)), device_id_type=MESH)
    pl.semaphore_signal(barrier, 1, device_id=(up_i, up_j), device_id_type=MESH)
    pl.semaphore_signal(barrier, 1, device_id=(down_i, down_j), device_id_type=MESH)

    def remote(source, target, place, device):
        return pltpu.make_async_remote_copy(
            src_ref=source, dst_ref=target, send_sem=send_sem.at[place],
            recv_sem=recv_sem.at[place], device_id=device, device_id_type=MESH,
        )

    def rows(number):
        return pl.ds(number * quarter, quarter)

    def roll_forward(source, target, base):
        copies = [
            remote(source.at[rows(0)], target.at[rows(3)], base, (down_i, down_j)),
            remote(source.at[rows(1)], target.at[rows(2)], base + 1, (down_i, j)),
            remote(source.at[rows(2)], target.at[rows(1)], base + 2, (i, down_j)),
        ]
        for copy in copies:
            copy.start()
        target[rows(0)] = source[rows(3)]
        return copies

    def roll_backward(source, target, base):
        copies = [
            remote(source.at[rows(3)], target.at[rows(0)], base, (up_i, up_j)),
            remote(source.at[rows(2)], target.at[rows(1)], base + 1, (up_i, j)),
            remote(source.at[rows(1)], target.at[rows(2)], base + 2, (i, up_j)),
        ]
        for copy in copies:
            copy.start()
        target[rows(3)] = source[rows(0)]
        return copies

    lane = lax.broadcasted_iota(jnp.int32, (heads, slots), 1)
    lane_row = lax.broadcasted_iota(jnp.int32, (1, slots), 1)
    channel = lax.broadcasted_iota(jnp.int32, (1, width), 1)
    head_masks = [
        ((channel >= h * head_size) & (channel < (h + 1) * head_size)).astype(F32).astype(BF16)
        for h in range(heads)
    ]
    pad_rows = 32

    def prepare_bias(k, occupied_row, coord_rows):
        cell = lax.broadcasted_iota(jnp.int32, (cells, slots), 0)
        blocks = [(jnp.broadcast_to(c, (cells, slots)) == cell).astype(F32) for c in coord_rows]
        empty = jnp.zeros((cells, slots), F32)
        first_row = cell == 0
        mask_block = jnp.where(
            first_row, jnp.broadcast_to(occupied_row.astype(F32) - 1.0, (cells, slots)), 0.0
        )
        one_block = jnp.where(first_row, 1.0, 0.0)
        rest = jnp.zeros((slots - 2 * pad_rows, slots), F32)
        right = jnp.concatenate(
            blocks + [one_block] + blocks + [empty, rest], axis=0
        ).astype(BF16)
        left = jnp.concatenate(blocks + [mask_block, empty, empty, empty, empty, rest], axis=0)
        left_t = jnp.transpose(left)
        onehot_s[k] = left_t.astype(BF16)
        onehot_t[k] = jnp.concatenate(blocks + [empty], axis=0).astype(BF16)
        table_pad[...] = jnp.zeros_like(table_pad)
        for e in range(3):
            table_pad[e, :, 0:span] = tables[k, e]
        mask_row = jnp.where(lane == 3 * cells, 1e30, 0.0)
        for u in range(cells):
            row = mask_row if u == 0 else jnp.zeros_like(mask_row)
            band[pl.ds(3 * cells + u, heads, stride=pad_rows), :] = row
        for e in range(3):
            padded = table_pad[e]
            inside = (lane >= e * cells) & (lane < (e + 1) * cells)
            for u in range(cells):
                shift = (e * cells + u - (cells - 1)) % slots
                moved = pltpu.roll(padded, shift, 1) if shift else padded
                tile = jnp.where(inside, moved, 0.0)
                high = tile.astype(BF16).astype(F32)
                tile = high + pltpu.roll(tile - high, pad_rows, 1)
                band[pl.ds(e * cells + u, heads, stride=pad_rows), :] = tile
        left_hot = onehot_s[k][:, 0:pad_rows]
        banded = jnp.concatenate(
            [band[h * pad_rows:(h + 1) * pad_rows, :] for h in range(heads)], axis=1
        ).astype(BF16)
        factors = dot_nn(left_hot, banded).astype(BF16)
        factors = jnp.concatenate(
            [factors[:, h * slots:(h + 1) * slots] for h in range(heads)], axis=0
        )
        left_bias[k] = dot_nn(factors, right)
        return left_t[:, 3 * cells:3 * cells + 1] + 1.0

    def stacked(values):
        return jnp.concatenate([values * head_masks[h] for h in range(heads)], axis=0)

    def attention_head(k, hidden):
        unit, rstd = norm_parts(hidden)
        unit_one[k] = unit
        rstd_one[k] = rstd
        normed = (unit * gains[k, 0:1]).astype(BF16)
        loads[1 + 4 * k].wait()
        projected = dot_nn(normed, wqkv_v[k])
        proj[k] = projected.astype(BF16)
        keys_t[k] = jnp.transpose(projected[:, width:2 * width]).astype(BF16)
        return jnp.transpose(projected[:, 2 * width:]).astype(BF16)

    def attention_part(k, hidden, values_t):
        queries = proj[k, :, 0:width]
        keys = proj[k, :, width:2 * width]
        scores_all = dot_nt(stacked(keys), queries)
        pieces = []
        for h in range(heads):
            here = slice(h * slots, (h + 1) * slots)
            scores = scores_all[here] * scale + left_bias[k, here]
            top = jnp.max(scores, axis=0, keepdims=True)
            powers = jnp.exp(scores - top)
            weights = (powers * (1.0 / jnp.sum(powers, axis=0, keepdims=True))).astype(BF16)
            probs[k, here] = weights
            pieces.append(dot_nn(values_t[h * head_size:(h + 1) * head_size], weights))
        mixed = jnp.transpose(jnp.concatenate(pieces, axis=0)).astype(BF16)
        loads[2 + 4 * k].wait()
        return hidden + dot_nn(mixed, wout_v[k])

    hidden_width = wup_v.shape[2]
    chunk = 2 * slots
    chunks = [pl.ds(start, chunk) for start in range(0, hidden_width, chunk)]

    def feed_part(k, middle, with_slope):
        unit, rstd = norm_parts(middle)
        unit_two[k] = unit
        rstd_two[k] = rstd
        normed = (unit * gains[k, 1:2]).astype(BF16)
        loads[3 + 4 * k].wait()
        for cut in chunks:
            wide = dot_nn(normed, wup_v[k, :, cut])
            square = wide * wide
            inner = jnp.tanh(wide * (GELU_SCALE + (GELU_SCALE * GELU_CUBE) * square))
            grown = 0.5 * (1.0 + inner)
            expanded_v[k, :, cut] = (wide * grown).astype(BF16)
            if with_slope:
                gelu_in[k, :, cut] = grown + wide * (0.5 * (1.0 - inner * inner)) * (
                    GELU_SCALE + (3.0 * GELU_SCALE * GELU_CUBE) * square
                )
            else:
                gelu_in[k, :, cut] = wide

    def feed_out(k, middle):
        loads[4 + 4 * k].wait()
        return (middle + dot_nn(expanded_v[k], wdown_v[k])).astype(BF16)

    def gelu_slope(k):
        for cut in chunks:
            wide = gelu_in[k, :, cut]
            square = wide * wide
            inner = jnp.tanh(wide * (GELU_SCALE + (GELU_SCALE * GELU_CUBE) * square))
            gelu_in[k, :, cut] = 0.5 * (1.0 + inner) + wide * (0.5 * (1.0 - inner * inner)) * (
                GELU_SCALE + (3.0 * GELU_SCALE * GELU_CUBE) * square
            )

    def stack_parts(k):
        q_stack[k] = stacked(proj[k, :, 0:width])
        v_stack[k] = stacked(proj[k, :, 2 * width:])

    def pull_wide(k, cotangent, with_slope):
        for cut in chunks:
            cot_wide = dot_nt(cotangent, wdown_v[k, cut, :]).astype(BF16)
            if with_slope:
                cot_wide = (cot_wide.astype(F32) * gelu_in[k, :, cut]).astype(BF16)
            cot_wide_v[k, :, cut] = cot_wide

    def scale_wide(k):
        for cut in chunks:
            cot_wide_v[k, :, cut] = (
                cot_wide_v[k, :, cut].astype(F32) * gelu_in[k, :, cut]
            ).astype(BF16)

    def pull_scores(k, cotangent):
        cot_normed = dot_nt(cot_wide_v[k], wup_v[k]).astype(BF16).astype(F32)
        cot_middle = cotangent.astype(F32) + norm_pullback(
            cot_normed, gains[k, 1:2], unit_two[k], rstd_two[k]
        )
        cot_mixed = dot_nt(cot_middle.astype(BF16), wout_v[k]).astype(BF16)
        mix_stack[...] = stacked(cot_mixed)
        cot_all = dot_nt(v_stack[k], cot_mixed)
        for h in range(heads):
            here = slice(h * slots, (h + 1) * slots)
            cot_probs = cot_all[here].astype(BF16).astype(F32)
            weights = probs[k, here].astype(F32)
            product = weights * cot_probs
            total = jnp.sum(product, axis=0, keepdims=True)
            high, low = split_two(product - weights * total)
            cot_pair[0:slots, here] = high
            cot_pair[slots:2 * slots, here] = low
        return cot_middle

    def table_sums(k):
        hot_twice = jnp.concatenate([onehot_s[k], onehot_s[k]], axis=0)
        hot_t_twice = jnp.concatenate([onehot_t[k], onehot_t[k]], axis=1)
        by_cell = dot_nn(hot_t_twice, cot_pair[...])
        by_cell = jnp.concatenate(
            [by_cell[:, h * slots:(h + 1) * slots] for h in range(heads)], axis=0
        )
        diag[...] = dot_nn(jnp.concatenate(split_two(by_cell), axis=1), hot_twice)
        sums = []
        for e in range(3):
            inside = (lane >= e * cells) & (lane < (e + 1) * cells)
            for u in range(cells):
                tile = jnp.where(inside, diag[pl.ds(e * cells + u, heads, stride=pad_rows), :], 0.0)
                shift = e * cells + (cells - 1) - u
                sums.append(pltpu.roll(tile, shift, 1) if shift else tile)
        while len(sums) > 1:
            sums = [a + b for a, b in zip(sums[0::2], sums[1::2])] + (
                [sums[-1]] if len(sums) % 2 else []
            )
        t_send[k * heads:(k + 1) * heads, :] = sums[0]

    def pull_proj(k):
        pieces = []
        for h in range(heads):
            high = cot_pair[0:slots, h * slots:(h + 1) * slots]
            pieces.append(dot_nn(keys_t[k, h * head_size:(h + 1) * head_size], high))
        cot_queries = (jnp.transpose(jnp.concatenate(pieces, axis=0)) * scale).astype(BF16)
        cot_keys = (dot_nn(cot_pair[0:slots, :], q_stack[k]) * scale).astype(BF16)
        probs_wide = jnp.concatenate(
            [probs[k, h * slots:(h + 1) * slots] for h in range(heads)], axis=1
        )
        cot_values = dot_nn(probs_wide, mix_stack[...]).astype(BF16)
        return jnp.concatenate([cot_queries, cot_keys, cot_values], axis=1)

    def pull_input(k, cot_proj, cot_middle):
        cot_normed = dot_nt(cot_proj, wqkv_v[k]).astype(BF16).astype(F32)
        return (
            cot_middle + norm_pullback(cot_normed, gains[k, 0:1], unit_one[k], rstd_one[k])
        ).astype(BF16)

    for n in (10, 11, 12, 13):
        loads[n].wait()
    meta[...] = jnp.zeros_like(meta)
    meta[0:1, :] = occ[0]
    for e in range(3):
        meta[e + 1:e + 2, :] = coords[0, e]
    loads[0].wait()
    hidden = x_v[...].astype(F32)
    values_t = attention_head(0, hidden)
    occupied = prepare_bias(0, occ[0], [coords[0, e] for e in range(3)])
    middle = attention_part(0, hidden, values_t)

    pl.semaphore_wait(barrier, nx + ny)
    meta_copies = [
        remote(meta, meta_recv.at[0], 0, (down_i, down_j)),
        remote(meta, meta_recv.at[1], 1, (down_i, j)),
        remote(meta, meta_recv.at[2], 2, (i, down_j)),
    ]
    for copy in meta_copies:
        copy.start()
    loads[9].wait()
    grad_copies = roll_forward(g_v, g_roll, 3)

    feed_part(0, middle, False)
    first[...] = feed_out(0, middle)
    first_copies = roll_forward(first, rolled, 6)

    for copy in meta_copies:
        copy.wait()
    own = pltpu.roll(meta[...], quarter, 1)
    from_y = pltpu.roll(meta_recv[2], slots - quarter, 1)
    from_x = pltpu.roll(meta_recv[1], quarter, 1)
    from_xy = pltpu.roll(meta_recv[0], slots - quarter, 1)
    moved = jnp.where(
        lane_row < quarter, own,
        jnp.where(lane_row < 2 * quarter, from_y, jnp.where(lane_row < 3 * quarter, from_x, from_xy)),
    )

    def wrapped(values):
        moved_on = values + half
        return jnp.where(moved_on >= cells, moved_on - cells, moved_on)

    shifted_occupied = prepare_bias(
        1, moved[0:1], [wrapped(moved[1:2]), wrapped(moved[2:3]), moved[3:4]]
    )
    gelu_slope(0)
    for copy in grad_copies:
        copy.wait()
    grad_in = (g_roll[...].astype(F32) * shifted_occupied).astype(BF16)
    loads[8].wait()
    pull_wide(1, grad_in, False)
    for copy in first_copies:
        copy.wait()
    hidden = rolled[...].astype(F32)
    middle = attention_part(1, hidden, attention_head(1, hidden))
    feed_part(1, middle, True)
    stack_parts(1)
    scale_wide(1)
    cot_middle = pull_scores(1, grad_in)
    grad_mid[...] = pull_input(1, pull_proj(1), cot_middle)
    mid_copies = roll_backward(grad_mid, grad_first, 12)
    second[...] = (middle + dot_nn(expanded_v[1], wdown_v[1])).astype(BF16)
    second_copies = roll_backward(second, back, 9)
    table_sums(1)
    stack_parts(0)
    for copy in mid_copies:
        copy.wait()

    def exchange(source, target, send, recv, me, count, device_of):
        copies = []
        for step in range(1, count):
            copies.append(
                pltpu.make_async_remote_copy(
                    src_ref=source, dst_ref=target.at[me], send_sem=send.at[step],
                    recv_sem=recv.at[step], device_id=device_of(lax.rem(me + step, count)),
                    device_id_type=MESH,
                )
            )
            copies[-1].start()
        target[me] = source[...]
        return copies

    cotangent = grad_first[...]
    pull_wide(0, cotangent, True)
    cot_middle = pull_scores(0, cotangent)
    table_sums(0)
    table_copies = exchange(t_send, t_recv_x, tx_send, tx_recv, i, nx, lambda other: (other, j))
    cot_proj = pull_proj(0)
    for copy in table_copies:
        copy.wait()
    total = t_recv_x[0]
    for n in range(1, nx):
        total = total + t_recv_x[n]
    t_mid[...] = total
    table_copies = exchange(t_mid, t_recv_y, ty_send, ty_recv, j, ny, lambda other: (i, other))
    grad_points[0, 0] = pull_input(0, cot_proj, cot_middle)
    for copy in second_copies:
        copy.wait()
    out_points[0, 0] = (back[...].astype(F32) * occupied).astype(BF16)
    for copy in table_copies:
        copy.wait()
    total = t_recv_y[0]
    for n in range(1, ny):
        total = total + t_recv_y[n]
    for k in range(2):
        for e in range(3):
            tile = total[k * heads:(k + 1) * heads]
            shift = (slots - 2 * cells * e) % slots
            tile = pltpu.roll(tile, shift, 1) if shift else tile
            grad_tables[k, e] = tile[:, 0:span]


def finish(points_in, grads_in, tables_in, points_out, grads_out, tables_out):
    points_out[...] = points_in[...]
    grads_out[...] = grads_in[...]
    tables_out[...] = tables_in[...]


def on_device(
    nx, ny, features, occupancy, coords, norm_gains, bias_tables, w_qkv, w_out, w_up, w_down, grad_out
):
    slots, width = features.shape[2:]
    coords = jnp.transpose(coords, (0, 2, 1, 3))
    heads = bias_tables.shape[2]
    hidden = w_up.shape[2]
    points = (slots, width)
    vmem = pl.BlockSpec(memory_space=pltpu.VMEM)
    hbm = pl.BlockSpec(memory_space=pltpu.HBM)
    dma = pltpu.SemaphoreType.DMA
    scratch = [
        pltpu.VMEM(occupancy.shape, jnp.int32),
        pltpu.VMEM(coords.shape, jnp.int32),
        pltpu.VMEM(norm_gains.shape, F32),
        pltpu.VMEM(bias_tables.shape, F32),
        pltpu.VMEM(points, BF16),
        pltpu.VMEM(points, BF16),
        pltpu.VMEM(w_qkv.shape, BF16),
        pltpu.VMEM(w_out.shape, BF16),
        pltpu.VMEM(w_up.shape, BF16),
        pltpu.VMEM(w_down.shape, BF16),
        pltpu.VMEM((8, slots), jnp.int32),
        pltpu.VMEM((3, 8, slots), jnp.int32),
    ]
    scratch += [pltpu.VMEM(points, BF16) for _ in range(7)]
    scratch += [
        pltpu.VMEM((3, heads, slots), F32),
        pltpu.VMEM((heads * 32, slots), F32),
        pltpu.VMEM((2, heads * slots, slots), F32),
        pltpu.VMEM((heads * 32, slots), F32),
        pltpu.VMEM((2, heads * slots, slots), BF16),
        pltpu.VMEM((2, slots, 3 * width), BF16),
        pltpu.VMEM((2, width, slots), BF16),
        pltpu.VMEM((2,) + points, F32),
        pltpu.VMEM((2,) + points, F32),
        pltpu.VMEM((2, slots, 1), F32),
        pltpu.VMEM((2, slots, 1), F32),
        pltpu.VMEM((2, slots, hidden), F32),
        pltpu.VMEM((2, slots, hidden), BF16),
        pltpu.VMEM((2, slots, hidden), BF16),
        pltpu.VMEM((2, slots, slots), BF16),
        pltpu.VMEM((2, 32, slots), BF16),
        pltpu.VMEM((2 * slots, heads * slots), BF16),
        pltpu.VMEM((2, heads * slots, width), BF16),
        pltpu.VMEM((2, heads * slots, width), BF16),
        pltpu.VMEM((heads * slots, width), BF16),
        pltpu.VMEM((2 * heads, slots), F32),
        pltpu.VMEM((nx, 2 * heads, slots), F32),
        pltpu.VMEM((2 * heads, slots), F32),
        pltpu.VMEM((ny, 2 * heads, slots), F32),
        dma((14,)), dma((15,)), dma((15,)), dma((nx,)), dma((nx,)), dma((ny,)), dma((ny,)),
    ]
    shapes = [(features.shape, BF16), (features.shape, BF16), (bias_tables.shape, F32)]
    padded_tables = 6 * 8 * slots * 4 * pl.cdiv(heads, 8)
    room = VMEM_BYTES - 4 * slots * width - padded_tables
    results = pl.pallas_call(
        partial(kernel, nx, ny),
        out_shape=[pltpu.VMEM(*shape) for shape in shapes],
        in_specs=[hbm] * 10,
        out_specs=[vmem] * 3,
        scratch_shapes=scratch,
        compiler_params=pltpu.CompilerParams(
            collective_id=0, has_side_effects=True, vmem_limit_bytes=room
        ),
    )(features, occupancy, coords, norm_gains, bias_tables, w_qkv, w_out, w_up, w_down, grad_out)
    return tuple(pl.pallas_call(
        finish,
        out_shape=[jax.ShapeDtypeStruct(*shape) for shape in shapes],
        in_specs=[vmem] * 3,
        out_specs=[vmem] * 3,
        compiler_params=pltpu.CompilerParams(vmem_limit_bytes=2 * 1024 * 1024),
    )(*results))


def solution(mesh):
    spread = P("gx", "gy", None, None)
    return jax.shard_map(
        partial(on_device, mesh.shape["gx"], mesh.shape["gy"]),
        mesh=mesh,
        in_specs=(spread, P("gx", "gy", None), spread, P(), P(), P(), P(), P(), P(), spread),
        out_specs=(spread, spread, P()),
        check_vma=False,
    )
```
